256 devices in a mesh: row: 8 (over x, y_lo), col: 16 (over z, core), depth: 2 (over y_hi).
Axes of the slice: x: 4, y: 4 (y_hi: 2, y_lo: 2; y = y_hi * 2 + y_lo), z: 8, core: 2. Of those that a mesh axis runs over, the one named last changes fastest.
Arguments:
- tokens: bfloat16 [2, 768, 8192], P('depth', None, ('col', 'row')), may hold values from -6 to 6
- gate_weight: bfloat16 [8192, 14336], P('col', 'row'), may hold values from -0.0625 to 0.0625
- up_weight: bfloat16 [8192, 14336], P('col', 'row'), may hold values from -0.0625 to 0.0625
- grad_hidden: bfloat16 [2, 768, 14336], P('depth', 'col', 'row'), may hold values from -0.75 to 0.75
Outputs:
- hidden: bfloat16 [2, 768, 14336], P('depth', 'col', 'row')
- grad_gate: float32 [8192, 14336], P('col', ('row', 'depth'))
- grad_up: float32 [8192, 14336], P('col', ('row', 'depth'))
The draws below stay inside these ranges and needn't reach their ends.
All inputs are finite; a program needn't handle non-finite values.
Results may differ from the reference program's by a relative error of at most 0.0034.
Values may be sent and summed in bfloat16 or wider, within the bound.
A program may use at most 128 MiB of HBM per device.

```python
import jax
import jax.numpy as jnp
from jax import lax

D = 8192
FF = 14336
MICRO = 2
SLAB = 768
N_COL = 16


def block_scale(rng, shape, shards, low, high):
    def one(position, blocks):
        draws = jax.random.uniform(jax.random.fold_in(jax.random.fold_in(rng, 6), position), (blocks,), jnp.float32, low / len(shards), high / len(shards))
        return jnp.repeat(jnp.exp(draws), shape[position] // blocks).reshape((-1,) + (1,) * (len(shape) - position - 1))

    loudness = one(*shards[0])
    for cut in shards[1:]:
        loudness = loudness * one(*cut)
    return loudness


def normal_values(own_key, shape, spread, most, cuts=(), held_as=jnp.bfloat16):
    loudness = block_scale(own_key, shape, cuts, -0.22, 0.18) if cuts else 1.0
    result = jax.random.normal(own_key, shape, jnp.float32) * spread * loudness
    return jnp.minimum(jnp.maximum(result, -most), most).astype(held_as)


def setup_inputs(seed: int = 0) -> dict:
    keys = jax.random.split(jax.random.key(seed), 5)
    return {
        "tokens": normal_values(keys[0], (MICRO, SLAB, D), 1.0, 6.0, ((0, 2), (2, 128))),
        "gate_weight": normal_values(keys[1], (D, FF), D ** -0.5, 0.0625, ((0, 16), (1, 8))),
        "up_weight": normal_values(keys[2], (D, FF), D ** -0.5, 0.0625, ((0, 16), (1, 8))),
        "grad_hidden": normal_values(keys[3], (MICRO, SLAB, FF), 0.05, 0.75, ((0, 2), (1, 16), (2, 8))),
    }


def reference(tokens, gate_weight, up_weight, grad_hidden):
    block_width = D // N_COL
    flat_tokens = tokens.reshape(MICRO * SLAB, D)

    def add_block(totals, index):
        offset = (index * block_width).astype(jnp.int32)
        picked = lax.dynamic_slice_in_dim(flat_tokens, offset, block_width, 1)
        gate_rows = lax.dynamic_slice_in_dim(gate_weight, offset, block_width, 0)
        up_rows = lax.dynamic_slice_in_dim(up_weight, offset, block_width, 0)
        gate_term = jnp.dot(picked, gate_rows, preferred_element_type=jnp.float32)
        up_term = jnp.dot(picked, up_rows, preferred_element_type=jnp.float32)
        return (totals[0] + gate_term, totals[1] + up_term), None

    zeros = jnp.zeros((MICRO * SLAB, FF), jnp.float32)
    totals, unused = lax.scan(add_block, (zeros, zeros), jnp.arange(N_COL, dtype=jnp.int32))
    gate_sum, up_sum = totals
    squash = jax.nn.sigmoid(gate_sum)
    hidden = (gate_sum * squash * up_sum).astype(jnp.bfloat16)
    cotangent = grad_hidden.reshape(MICRO * SLAB, FF).astype(jnp.float32)
    gate_act = (cotangent * up_sum * squash * (1.0 + gate_sum * (1.0 - squash))).astype(jnp.bfloat16)
    up_act = (cotangent * gate_sum * squash).astype(jnp.bfloat16)
    dims = (((0,), (0,)), ((), ()))
    grad_gate = lax.dot_general(flat_tokens, gate_act, dims, preferred_element_type=jnp.float32)
    grad_up = lax.dot_general(flat_tokens, up_act, dims, preferred_element_type=jnp.float32)
    return hidden.reshape(MICRO, SLAB, FF), grad_gate, grad_up
```

```python
import functools

import jax
import jax.numpy as jnp
from jax import lax
from jax.experimental import pallas as pl
from jax.experimental.pallas import tpu as pltpu
from jax.sharding import PartitionSpec as P

MESH = pl.DeviceIdType.MESH
BF = jnp.bfloat16
F32 = jnp.float32
OFFSETS = (4, 3, -3, 2, -2, 1, -1, 0)
SLOT = {offset: slot for slot, offset in enumerate(OFFSETS)}
GROUPS = ((0, 1), (1, 3), (3, 8))
CHUNKS = ((0, 512), (512, 384))
HOPS = ({1: 4, -1: 3}, {1: 3, -1: 4})
ROWS = 48
HALF = 896
SCALE = 2.0**18


def encode(x):
    t = x * SCALE
    u = t * t
    return (u * t * jnp.abs(t)).astype(BF)


def decode(y):
    y = y.astype(F32)
    r = lax.rsqrt(lax.rsqrt(jnp.abs(y))) * (1.0 / SCALE)
    return jnp.where(y < 0.0, -r, r)


def kernel(
    tok_hbm, wg_hbm, wu_hbm, gh_hbm, hid_hbm, gg_hbm, gu_hbm,
    tok, wg, wu, gh, hid, gg, gu,
    pk, pkr, pko, tk, tkt, part, frm,
    rs_send0, rs_send1, rs_recv0, rs_recv1, act0, act1, g0, g1,
    load_sem, out_sem, tok_send, tok_recv, oth_send, oth_recv, part_send, part_recv,
    rs_ssem, rs_rsem, swap_send, swap_recv, ag_send, ag_recv, fwd_send, fwd_recv,
):
    row = lax.axis_index("row")
    col = lax.axis_index("col")
    dep = lax.axis_index("depth")
    z = col // 2
    core = col % 2
    other = 1 - core
    rs_send, rs_recv = (rs_send0, rs_send1), (rs_recv0, rs_recv1)
    act, g = (act0, act1), (g0, g1)
    waits = []

    def at(row_=None, z_=None, core_=None, dep_=None):
        return {
            "row": row if row_ is None else row_,
            "col": (z if z_ is None else z_) * 2 + (core if core_ is None else core_),
            "depth": dep if dep_ is None else dep_,
        }

    def along(step):
        return at(z_=lax.rem(z + step + 8, 8))

    def remote(src, dst, send, recv, device):
        return pltpu.make_async_remote_copy(
            src_ref=src, dst_ref=dst, send_sem=send, recv_sem=recv, device_id=device, device_id_type=MESH
        )

    def push(src, dst, send, recv, device):
        copy = remote(src, dst, send, recv, device)
        copy.start()
        waits.append(copy)

    loads = [
        pltpu.make_async_copy(tok_hbm.at[0], tok, load_sem.at[0]),
        pltpu.make_async_copy(wg_hbm, wg, load_sem.at[1]),
        pltpu.make_async_copy(wu_hbm, wu, load_sem.at[2]),
        pltpu.make_async_copy(gh_hbm.at[0], gh, load_sem.at[3]),
    ]
    for load in loads:
        load.start()

    barrier = pltpu.get_barrier_semaphore()
    peers = [at(row_=lax.rem(row + k, 8)) for k in range(1, 8)]
    peers += [at(row_=lax.rem(row + k, 8), dep_=1 - dep) for k in range(8)]
    peers += [along(1), along(-1), at(core_=other)]
    for peer in peers:
        pl.semaphore_signal(barrier, inc=1, device_id=peer, device_id_type=MESH)

    loads[0].wait()
    for slot, offset in enumerate(OFFSETS):
        first = pl.multiple_of(lax.rem(z + offset + 8, 8) * 96, 32)
        low = tok[pl.ds(first, ROWS), :]
        high = tok[pl.ds(pl.multiple_of(first + ROWS, 16), ROWS), :]
        both = jnp.concatenate([low, high], axis=1)
        pk[slot] = both
        pkr[row, slot] = both
    pl.semaphore_wait(barrier, len(peers))

    for n, (lo, hi) in enumerate(GROUPS):
        for k in range(1, 8):
            push(
                pk.at[pl.ds(lo, hi - lo)], pkr.at[row, pl.ds(lo, hi - lo)],
                tok_send.at[n, k], tok_recv.at[n, row], at(row_=lax.rem(row + k, 8)),
            )
    for k in range(8):
        push(pk, pko.at[row], oth_send.at[k], oth_recv.at[row], at(row_=lax.rem(row + k, 8), dep_=1 - dep))

    def wait_tokens(n):
        lo, hi = GROUPS[n]
        for k in range(1, 8):
            src = lax.rem(row + k, 8)
            remote(
                pk.at[pl.ds(lo, hi - lo)], pkr.at[src, pl.ds(lo, hi - lo)],
                tok_send.at[n, k], tok_recv.at[n, src], at(row_=src),
            ).wait_recv()

    def unpack(packed, slot, which):
        for m in range(4):
            a = packed[2 * m, slot]
            b = packed[2 * m + 1, slot]
            for c in range(2):
                lanes = slice(64 * c, 64 * c + 64)
                tk[slot, c, which, :, 128 * m : 128 * m + 128] = jnp.concatenate([a[:, lanes], b[:, lanes]], axis=1)

    def project(slot):
        unpack(pkr, slot, 0)
        lhs = jnp.concatenate([tk[slot, 0, 0], tk[slot, 1, 0]], axis=0)
        for q in range(4):
            w = (wg, wu)[q // 2][:, HALF * (q % 2) : HALF * (q % 2) + HALF]
            res = jnp.dot(lhs, w, preferred_element_type=F32)
            part[0, slot, q] = res[:ROWS]
            part[1, slot, q] = res[ROWS:]

    def to_partner(slot):
        push(part.at[other, slot], frm.at[slot], part_send.at[slot], part_recv.at[slot], at(core_=other))

    def from_partner(slot):
        remote(part.at[other, slot], frm.at[slot], part_send.at[slot], part_recv.at[slot], at(core_=other)).wait_recv()

    def project_all(lo, hi):
        if hi - lo == 1:
            project(lo)
        else:
            pl.loop(lo, hi)(project)
        for slot in range(lo, hi):
            to_partner(slot)

    def rs_copy(i, way, j):
        d = 0 if way == 1 else 1
        return remote(
            rs_send[i].at[d, j - 1], rs_recv[i].at[d, j - 1], rs_ssem.at[i, d, j - 1], rs_rsem.at[i, d, j - 1], along(way)
        )

    def rs_step(i, way, j):
        d = 0 if way == 1 else 1
        slot = SLOT[way * j] if j < 4 else 0
        t0, w = CHUNKS[i]
        arrived = j < HOPS[i][way]
        if arrived:
            rs_copy(i, way, j + 1).wait_recv()

        @pl.loop(0, 12)
        def _(it):
            q = it // 3
            rows = pl.ds(pl.multiple_of(it % 3 * 16, 16), 16)
            x = part[core, slot, q, rows, t0 : t0 + w] + frm[slot, q, rows, t0 : t0 + w]
            if arrived:
                x = x + decode(rs_recv[i][d, j, q, rows, :])
            rs_send[i][d, j - 1, q, rows, :] = encode(x)

        copy = rs_copy(i, way, j)
        copy.start()
        waits.append(copy)

    loads[1].wait()
    loads[2].wait()
    wait_tokens(0)
    project_all(0, 1)
    wait_tokens(1)
    project_all(1, 3)
    from_partner(0)
    rs_step(0, 1, 4)
    rs_step(1, -1, 4)
    from_partner(1)
    from_partner(2)
    rs_step(1, 1, 3)
    rs_step(0, -1, 3)
    wait_tokens(2)
    project_all(3, 5)
    rs_step(0, 1, 3)
    rs_step(1, -1, 3)
    from_partner(3)
    from_partner(4)
    rs_step(1, 1, 2)
    rs_step(0, -1, 2)
    project_all(5, 7)
    rs_step(0, 1, 2)
    rs_step(1, -1, 2)
    from_partner(5)
    from_partner(6)
    rs_step(1, 1, 1)
    rs_step(0, -1, 1)
    project_all(7, 8)
    rs_step(0, 1, 1)
    rs_step(1, -1, 1)
    from_partner(7)

    for k in range(8):
        src = lax.rem(row + k, 8)
        remote(pk, pko.at[src], oth_send.at[k], oth_recv.at[src], at(row_=src, dep_=1 - dep)).wait_recv()

    @pl.loop(0, 8)
    def _(slot):
        unpack(pko, slot, 1)

    for m in range(12):
        rows = tk[...].reshape(1536, 512)[128 * m : 128 * m + 128, :]
        tkt[:, 128 * m : 128 * m + 128] = rows.T

    loads[3].wait()

    def acts(i):
        t0, w = CHUNKS[i]
        rs_copy(i, 1, 1).wait_recv()
        rs_copy(i, -1, 1).wait_recv()

        def total(q, rows):
            x = part[core, 7, q, rows, t0 : t0 + w] + frm[7, q, rows, t0 : t0 + w]
            return x + decode(rs_recv[i][0, 0, q, rows, :]) + decode(rs_recv[i][1, 0, q, rows, :])

        for half in range(2):
            for r in range(3):
                rows = slice(16 * r, 16 * r + 16)
                cols = slice(HALF * half + t0, HALF * half + t0 + w)
                gate = total(half, rows)
                up = total(2 + half, rows)
                squash = jax.nn.sigmoid(gate)
                hid[rows, cols] = (gate * squash * up).astype(BF)
                cot = gh[rows, cols].astype(F32)
                act[i][half, rows, 0:w] = (cot * up * squash * (1.0 + gate * (1.0 - squash))).astype(BF)
                act[i][half, rows, w : 2 * w] = (cot * gate * squash).astype(BF)
        push(act[i].at[1 - dep], g[i].at[14 + core, 1], swap_send.at[i], swap_recv.at[i], at(dep_=1 - dep))
        g[i][14 + core, 0] = act[i][dep]

    def ag_copy(i, way, hop):
        d = 0 if way == 1 else 1
        src = SLOT[-way * (hop - 1)]
        dst = SLOT[-way * hop] if hop < 4 else 0
        return remote(
            g[i].at[2 * src + core], g[i].at[2 * dst + core], ag_send.at[i, d, hop - 1], ag_recv.at[i, d, hop - 1], along(way)
        )

    def fwd_copy(i, slot):
        return remote(
            g[i].at[2 * slot + core], g[i].at[2 * slot + core], fwd_send.at[i, slot], fwd_recv.at[i, slot], at(core_=other)
        )

    def start(copy):
        copy.start()
        waits.append(copy)

    def first(i):
        remote(
            act[i].at[1 - dep], g[i].at[14 + core, 1], swap_send.at[i], swap_recv.at[i], at(dep_=1 - dep)
        ).wait_recv()
        start(ag_copy(i, 1, 1))
        start(ag_copy(i, -1, 1))
        start(fwd_copy(i, 7))

    def onward(i, way, hop):
        ag_copy(i, way, hop).wait_recv()
        if hop < HOPS[i][way]:
            start(ag_copy(i, way, hop + 1))
        start(fwd_copy(i, SLOT[-way * hop] if hop < 4 else 0))

    acts(0)
    acts(1)
    first(0)
    first(1)
    for hop in range(1, 4):
        for i in range(2):
            onward(i, 1, hop)
            onward(i, -1, hop)
    onward(0, 1, 4)
    onward(1, -1, 4)
    hid_out = pltpu.make_async_copy(hid, hid_hbm.at[0], out_sem.at[0])
    hid_out.start()
    for i in range(2):
        for slot in range(8):
            remote(
                g[i].at[2 * slot + other], g[i].at[2 * slot + other], fwd_send.at[i, slot], fwd_recv.at[i, slot], at(core_=other)
            ).wait_recv()

    for i in range(2):
        t0, w = CHUNKS[i]
        for k, out in enumerate((gg, gu)):
            for n in range(0, w, 128):
                rhs = g[i][:, :, :, k * w + n : k * w + n + 128].reshape(1536, 128)
                out[:, t0 + n : t0 + n + 128] = jnp.dot(tkt[...], rhs, preferred_element_type=F32)
    outs = [pltpu.make_async_copy(gg, gg_hbm, out_sem.at[1]), pltpu.make_async_copy(gu, gu_hbm, out_sem.at[2])]
    for out in outs:
        out.start()
    for copy in waits:
        copy.wait_send()
    hid_out.wait()
    for out in outs:
        out.wait()


def local(tokens, gate_weight, up_weight, grad_hidden):
    dma = pltpu.SemaphoreType.DMA
    v = pltpu.VMEM
    any_spec = pl.BlockSpec(memory_space=pl.ANY)
    w0, w1 = CHUNKS[0][1], CHUNKS[1][1]
    return pl.pallas_call(
        kernel,
        out_shape=(
            jax.ShapeDtypeStruct((1, 48, 1792), BF),
            jax.ShapeDtypeStruct((512, 896), F32),
            jax.ShapeDtypeStruct((512, 896), F32),
        ),
        in_specs=[any_spec] * 4,
        out_specs=(any_spec,) * 3,
        scratch_shapes=[
            v((768, 64), BF), v((512, 1792), BF), v((512, 1792), BF), v((48, 1792), BF),
            v((48, 1792), BF), v((512, 896), F32), v((512, 896), F32),
            v((8, 48, 128), BF), v((8, 8, 48, 128), BF), v((8, 8, 48, 128), BF),
            v((8, 2, 2, 48, 512), BF), v((512, 1536), BF),
            v((2, 8, 4, 48, 896), F32), v((8, 4, 48, 896), F32),
            v((2, 4, 4, 48, w0), BF), v((2, 4, 4, 48, w1), BF),
            v((2, 4, 4, 48, w0), BF), v((2, 4, 4, 48, w1), BF),
            v((2, 48, 2 * w0), BF), v((2, 48, 2 * w1), BF),
            v((16, 2, 48, 2 * w0), BF), v((16, 2, 48, 2 * w1), BF),
            dma((4,)), dma((3,)), dma((3, 8)), dma((3, 8)), dma((8,)), dma((8,)), dma((8,)), dma((8,)),
            dma((2, 2, 4)), dma((2, 2, 4)), dma((2,)), dma((2,)), dma((2, 2, 4)), dma((2, 2, 4)), dma((2, 8)), dma((2, 8)),
        ],
        compiler_params=pltpu.CompilerParams(collective_id=0, has_side_effects=True, vmem_limit_bytes=60 << 20),
    )(tokens, gate_weight, up_weight, grad_hidden)


def solution(mesh):
    in_specs = (
        P("depth", None, ("col", "row")),
        P("col", "row"),
        P("col", "row"),
        P("depth", "col", "row"),
    )
    out_specs = (P("depth", "col", "row"), P("col", ("row", "depth")), P("col", ("row", "depth")))
    return jax.shard_map(local, mesh=mesh, in_specs=in_specs, out_specs=out_specs, check_vma=False)
```

```python
import jax
import jax.numpy as jnp
from jax import lax
from jax.experimental import pallas as pl
from jax.experimental.pallas import tpu as pltpu
from jax.sharding import PartitionSpec as P

MESH = pl.DeviceIdType.MESH
BF = jnp.bfloat16
F32 = jnp.float32
OFFSETS = (4, 3, -3, 2, -2, 1, -1, 0)
SLOT = {offset: slot for slot, offset in enumerate(OFFSETS)}
GROUPS = ((0, 1), (1, 3), (3, 5), (5, 7), (7, 8))
ROWS = 48
HALF = 896
SCALE = 2.0**18
CHUNKS = ((0, 128), (128, 128), (256, 256), (512, 384))
HOPS = ({1: 4, -1: 3}, {1: 4, -1: 3}, {1: 3, -1: 4}, {1: 3, -1: 4})

ORDER = (
    ("P", 0), ("P", 1), ("R", 0, 1, 4), ("R", 1, 1, 4), ("R", 2, -1, 4), ("P", 2), ("R", 0, -1, 3), ("R", 1, -1, 3),
    ("R", 2, 1, 3), ("R", 3, -1, 4), ("R", 0, 1, 3), ("P", 3), ("P", 4), ("X",), ("R", 0, -1, 2), ("R", 1, 1, 3),
    ("R", 1, -1, 2), ("R", 2, -1, 3), ("R", 0, 1, 2), ("R", 2, 1, 2), ("R", 3, -1, 3), ("R", 3, 1, 3),
    ("R", 0, -1, 1), ("R", 0, 1, 1), ("R", 1, -1, 1), ("R", 1, 1, 2), ("R", 2, -1, 2), ("R", 2, 1, 1),
    ("R", 3, -1, 2), ("R", 3, 1, 2), ("A", 0), ("T", 3), ("R", 1, 1, 1), ("T", 2), ("T", 1), ("R", 2, -1, 1),
    ("T", 0), ("N", 0, 1, 0), ("N", 0, -1, 0), ("R", 3, -1, 1), ("R", 3, 1, 1), ("A", 1), ("A", 2), ("N", 0, 1, 1),
    ("N", 0, -1, 1), ("W", 0, 3), ("N", 1, 1, 0), ("N", 1, -1, 0), ("A", 3), ("N", 2, -1, 0), ("N", 2, 1, 0),
    ("N", 0, -1, 2), ("N", 0, 1, 2), ("W", 0, 2), ("N", 1, 1, 1), ("N", 1, -1, 1), ("W", 1, 3), ("N", 3, -1, 0),
    ("N", 3, 1, 0), ("N", 2, -1, 1), ("N", 2, 1, 1), ("N", 0, -1, 3), ("W", 2, 3), ("N", 1, -1, 2), ("N", 1, 1, 2),
    ("N", 0, 1, 3), ("W", 1, 2), ("N", 3, -1, 1), ("N", 3, 1, 1), ("W", 0, 1), ("W", 3, 3), ("N", 2, -1, 2),
    ("N", 2, 1, 2), ("N", 1, -1, 3), ("N", 0, 1, 4), ("W", 2, 2), ("N", 1, 1, 3), ("W", 0, 0), ("N", 3, -1, 2),
    ("W", 1, 1), ("N", 3, 1, 2), ("N", 2, -1, 3), ("W", 3, 2), ("N", 2, 1, 3), ("N", 1, 1, 4), ("W", 2, 1),
    ("N", 3, -1, 3), ("W", 1, 0), ("N", 3, 1, 3), ("N", 2, -1, 4), ("W", 3, 1), ("W", 2, 0), ("N", 3, -1, 4),
    ("W", 3, 0),
)


def encode(x):
    t = x * SCALE
    u = t * t
    return (u * t * jnp.abs(t)).astype(BF)


def decode(y):
    y = y.astype(F32)
    r = lax.rsqrt(lax.rsqrt(jnp.abs(y))) * (1.0 / SCALE)
    return jnp.where(y < 0.0, -r, r)


def kernel(tok_hbm, wg_hbm, wu_hbm, gh_hbm, hid_hbm, gg_hbm, gu_hbm, *scratch):
    n = len(CHUNKS)
    (tokt, tok, wg, wu, gh, hid, gg, gu, pk, pkr, pko, tk, tkt, part, frm), scratch = scratch[:15], scratch[15:]
    rs_send, rs_recv, act, g = (scratch[i * n : i * n + n] for i in range(4))
    (
        load_sem, out_sem, tok_send, tok_recv, oth_send, oth_recv, part_send, part_recv,
        rs_ssem, rs_rsem, swap_send, swap_recv, ag_send, ag_recv, fwd_send, fwd_recv,
    ) = scratch[4 * n :]
    row = lax.axis_index("row")
    col = lax.axis_index("col")
    dep = lax.axis_index("depth")
    z = col // 2
    core = col % 2
    other = 1 - core
    sent = []
    written = []

    def at(row_=None, z_=None, core_=None, dep_=None):
        return {
            "row": row if row_ is None else row_,
            "col": (z if z_ is None else z_) * 2 + (core if core_ is None else core_),
            "depth": dep if dep_ is None else dep_,
        }

    def along(step):
        return at(z_=lax.rem(z + step + 8, 8))

    def remote(src, dst, send, recv, device):
        return pltpu.make_async_remote_copy(
            src_ref=src, dst_ref=dst, send_sem=send, recv_sem=recv, device_id=device, device_id_type=MESH
        )

    def start(copy):
        copy.start()
        sent.append(copy)

    loads = [
        pltpu.make_async_copy(tok_hbm, tokt, load_sem.at[0]),
        pltpu.make_async_copy(wg_hbm, wg, load_sem.at[1]),
        pltpu.make_async_copy(wu_hbm, wu, load_sem.at[2]),
        pltpu.make_async_copy(gh_hbm.at[0], gh, load_sem.at[3]),
    ]
    for load in loads:
        load.start()

    barrier = pltpu.get_barrier_semaphore()
    peers = [at(row_=lax.rem(row + k, 8)) for k in range(1, 8)]
    peers += [at(row_=lax.rem(row + k, 8), dep_=1 - dep) for k in range(8)]
    peers += [along(1), along(-1), at(core_=other)]
    for peer in peers:
        pl.semaphore_signal(barrier, inc=1, device_id=peer, device_id_type=MESH)

    loads[0].wait()
    for m in range(6):
        tok[128 * m : 128 * m + 128, :] = tokt[:, 128 * m : 128 * m + 128].T
    for slot, offset in enumerate(OFFSETS):
        first = pl.multiple_of(lax.rem(z + offset + 8, 8) * 96, 32)
        low = tok[pl.ds(first, ROWS), :]
        high = tok[pl.ds(pl.multiple_of(first + ROWS, 16), ROWS), :]
        both = jnp.concatenate([low, high], axis=1)
        pk[slot] = both
        pkr[row, slot] = both
    pl.semaphore_wait(barrier, len(peers))

    def tok_copy(m, k, src):
        span = pl.ds(GROUPS[m][0], GROUPS[m][1] - GROUPS[m][0])
        return remote(pk.at[span], pkr.at[src, span], tok_send.at[m, k], tok_recv.at[m, src], at(row_=lax.rem(row + k, 8)))

    def oth_copy(k, src):
        return remote(pk, pko.at[src], oth_send.at[k], oth_recv.at[src], at(row_=lax.rem(row + k, 8), dep_=1 - dep))

    def part_copy(slot):
        return remote(part.at[other, slot], frm.at[slot], part_send.at[slot], part_recv.at[slot], at(core_=other))

    def rs_copy(i, way, j):
        d = 0 if way == 1 else 1
        return remote(
            rs_send[i].at[d, j - 1], rs_recv[i].at[d, j - 1], rs_ssem.at[i, d, j - 1], rs_rsem.at[i, d, j - 1], along(way)
        )

    def swap_copy(i):
        return remote(act[i].at[1 - dep], g[i].at[14 + core, 1], swap_send.at[i], swap_recv.at[i], at(dep_=1 - dep))

    def ag_copy(i, way, hop):
        d = 0 if way == 1 else 1
        src = SLOT[-way * (hop - 1)]
        dst = SLOT[-way * hop] if hop < 4 else 0
        return remote(
            g[i].at[2 * src + core], g[i].at[2 * dst + core], ag_send.at[i, d, hop - 1], ag_recv.at[i, d, hop - 1], along(way)
        )

    def fwd_copy(i, slot, whose):
        block = g[i].at[2 * slot + whose]
        return remote(block, block, fwd_send.at[i, slot], fwd_recv.at[i, slot], at(core_=other))

    def unpack(packed, slot, which):
        for m in range(4):
            a = packed[2 * m, slot]
            b = packed[2 * m + 1, slot]
            for c in range(2):
                lanes = slice(64 * c, 64 * c + 64)
                tk[slot, c, which, :, 128 * m : 128 * m + 128] = jnp.concatenate([a[:, lanes], b[:, lanes]], axis=1)

    def project(slot):
        unpack(pkr, slot, 0)
        lhs = jnp.concatenate([tk[slot, 0, 0], tk[slot, 1, 0]], axis=0)
        for q in range(4):
            w = (wg, wu)[q // 2][:, HALF * (q % 2) : HALF * (q % 2) + HALF]
            res = jnp.dot(lhs, w, preferred_element_type=F32)
            part[0, slot, q] = res[:ROWS]
            part[1, slot, q] = res[ROWS:]

    arrived_parts = set()

    def need_part(slot):
        if slot not in arrived_parts:
            arrived_parts.add(slot)
            part_copy(slot).wait_recv()

    def step_p(m):
        lo, hi = GROUPS[m]
        if m == 0:
            loads[1].wait()
            loads[2].wait()
        for k in range(1, 8):
            tok_copy(m, k, lax.rem(row + k, 8)).wait_recv()
        if hi - lo == 1:
            project(lo)
        else:
            pl.loop(lo, hi)(project)
        for slot in range(lo, hi):
            start(part_copy(slot))

    def step_x():
        for k in range(8):
            start(oth_copy(k, row))

    unpacked = []

    def step_t(kg):
        if not unpacked:
            for k in range(8):
                oth_copy(k, lax.rem(row + k, 8)).wait_recv()
        unpacked.append(kg)
        for slot in (2 * kg, 2 * kg + 1):
            unpack(pko, slot, 1)
        rows = tk[2 * kg : 2 * kg + 2].reshape(384, 512)
        for m in range(3):
            tkt[:, 384 * kg + 128 * m : 384 * kg + 128 * m + 128] = rows[128 * m : 128 * m + 128, :].T

    def step_r(i, way, j):
        d = 0 if way == 1 else 1
        slot = SLOT[way * j] if j < 4 else 0
        t0, w = CHUNKS[i]
        arrived = j < HOPS[i][way]
        need_part(slot)
        if arrived:
            rs_copy(i, way, j + 1).wait_recv()

        @pl.loop(0, 12)
        def _(it):
            q = it // 3
            rows = pl.ds(pl.multiple_of(it % 3 * 16, 16), 16)
            x = part[core, slot, q, rows, t0 : t0 + w] + frm[slot, q, rows, t0 : t0 + w]
            if arrived:
                x = x + decode(rs_recv[i][d, j, q, rows, :])
            rs_send[i][d, j - 1, q, rows, :] = encode(x)

        start(rs_copy(i, way, j))

    def step_a(i):
        t0, w = CHUNKS[i]
        need_part(7)
        rs_copy(i, 1, 1).wait_recv()
        rs_copy(i, -1, 1).wait_recv()
        if loads[3] is not None:
            loads[3].wait()
            loads[3] = None

        def total(q, rows):
            x = part[core, 7, q, rows, t0 : t0 + w] + frm[7, q, rows, t0 : t0 + w]
            return x + decode(rs_recv[i][0, 0, q, rows, :]) + decode(rs_recv[i][1, 0, q, rows, :])

        @pl.loop(0, 3)
        def _(r):
            rows = pl.ds(pl.multiple_of(r * 16, 16), 16)
            for half in range(2):
                cols = slice(HALF * half + t0, HALF * half + t0 + w)
                gate = total(half, rows)
                up = total(2 + half, rows)
                squash = jax.nn.sigmoid(gate)
                hid[rows, cols] = (gate * squash * up).astype(BF)
                cot = gh[rows, cols].astype(F32)
                act[i][half, rows, 0:w] = (cot * up * squash * (1.0 + gate * (1.0 - squash))).astype(BF)
                act[i][half, rows, w : 2 * w] = (cot * gate * squash).astype(BF)

        start(swap_copy(i))
        g[i][14 + core, 0] = act[i][dep]

    begun = set()

    def step_n(i, way, hop):
        if hop == 0:
            if i not in begun:
                swap_copy(i).wait_recv()
        else:
            ag_copy(i, way, hop).wait_recv()
        if hop < HOPS[i][way]:
            start(ag_copy(i, way, hop + 1))
        if hop or i not in begun:
            start(fwd_copy(i, SLOT[-way * hop] if hop < 4 else 0, core))
        begun.add(i)

    summed = {}

    def step_w(i, kg):
        t0, w = CHUNKS[i]
        for slot in (2 * kg, 2 * kg + 1):
            fwd_copy(i, slot, other).wait_recv()
        first = i not in summed
        summed[i] = summed.get(i, 0) + 1

        @pl.loop(0, 2)
        def _(half):
            rows = pl.ds(pl.multiple_of(half * 256, 256), 256)
            lhs = tkt[rows, 384 * kg : 384 * kg + 384]
            for tile in range(0, 2 * w // 128, 2):
                rhs = g[i][4 * kg : 4 * kg + 4, :, :, 128 * tile : 128 * tile + 256].reshape(384, 256)
                res = jnp.dot(lhs, rhs, preferred_element_type=F32)
                for k in range(2):
                    out, c = (gg, tile + k) if tile + k < w // 128 else (gu, tile + k - w // 128)
                    cols = slice(t0 + 128 * c, t0 + 128 * c + 128)
                    piece = res[:, 128 * k : 128 * k + 128]
                    out[rows, cols] = piece if first else out[rows, cols] + piece

        if summed[i] == 4:
            for k, (src, dst) in enumerate(((gg, gg_hbm), (gu, gu_hbm))):
                copy = pltpu.make_async_copy(src.at[:, t0 : t0 + w], dst.at[:, t0 : t0 + w], out_sem.at[2 * i + k])
                copy.start()
                written.append(copy)

    for m in range(len(GROUPS)):
        for k in range(1, 8):
            start(tok_copy(m, k, row))
    steps = {"P": step_p, "X": step_x, "T": step_t, "R": step_r, "A": step_a, "N": step_n, "W": step_w}
    for name, *args in ORDER:
        steps[name](*args)
    out = pltpu.make_async_copy(hid, hid_hbm.at[0], out_sem.at[2 * n])
    out.start()
    for copy in sent:
        copy.wait_send()
    for copy in written:
        copy.wait()
    out.wait()


def local(tokens, gate_weight, up_weight, grad_hidden):
    dma = pltpu.SemaphoreType.DMA
    v = pltpu.VMEM
    any_spec = pl.BlockSpec(memory_space=pl.ANY)
    n = len(CHUNKS)
    widths = [w for _, w in CHUNKS]
    return pl.pallas_call(
        kernel,
        out_shape=(
            jax.ShapeDtypeStruct((1, 48, 1792), BF),
            jax.ShapeDtypeStruct((512, 896), F32),
            jax.ShapeDtypeStruct((512, 896), F32),
        ),
        in_specs=[any_spec] * 4,
        out_specs=(any_spec,) * 3,
        scratch_shapes=[
            v((64, 768), BF), v((768, 64), BF), v((512, 1792), BF), v((512, 1792), BF), v((48, 1792), BF),
            v((48, 1792), BF), v((512, 896), F32), v((512, 896), F32),
            v((8, 48, 128), BF), v((8, 8, 48, 128), BF), v((8, 8, 48, 128), BF),
            v((8, 2, 2, 48, 512), BF), v((512, 1536), BF),
            v((2, 8, 4, 48, 896), F32), v((8, 4, 48, 896), F32),
            *[v((2, 4, 4, 48, w), BF) for w in widths],
            *[v((2, 4, 4, 48, w), BF) for w in widths],
            *[v((2, 48, 2 * w), BF) for w in widths],
            *[v((16, 2, 48, 2 * w), BF) for w in widths],
            dma((4,)), dma((2 * n + 1,)), dma((5, 8)), dma((5, 8)), dma((8,)), dma((8,)), dma((8,)), dma((8,)),
            dma((n, 2, 4)), dma((n, 2, 4)), dma((n,)), dma((n,)), dma((n, 2, 4)), dma((n, 2, 4)), dma((n, 8)), dma((n, 8)),
        ],
        compiler_params=pltpu.CompilerParams(collective_id=0, has_side_effects=True, vmem_limit_bytes=60 << 20),
    )(tokens[0].T, gate_weight, up_weight, grad_hidden)


def solution(mesh):
    in_specs = (
        P("depth", None, ("col", "row")),
        P("col", "row"),
        P("col", "row"),
        P("depth", "col", "row"),
    )
    out_specs = (P("depth", "col", "row"), P("col", ("row", "depth")), P("col", ("row", "depth")))
    return jax.shard_map(local, mesh=mesh, in_specs=in_specs, out_specs=out_specs, check_vma=False)
```

```python
import jax
import jax.numpy as jnp
from jax import lax
from jax.experimental import pallas as pl
from jax.experimental.pallas import tpu as pltpu
from jax.sharding import PartitionSpec as P

MESH = pl.DeviceIdType.MESH
BF = jnp.bfloat16
F32 = jnp.float32
OFFSETS = (4, 3, -3, 2, -2, 1, -1, 0)
SLOT = {offset: slot for slot, offset in enumerate(OFFSETS)}
GROUPS = ((0, 1), (1, 3), (3, 5), (5, 7), (7, 8))
ROWS = 48
HALF = 896
SCALE = 2.0**18
CHUNKS = ((0, 128), (128, 128), (256, 256), (512, 256), (768, 128))
HOPS = ({1: 4, -1: 3}, {1: 4, -1: 3}, {1: 4, -1: 3}, {1: 3, -1: 4}, {1: 3, -1: 4})

ORDER = (
    ("Q", 0), ("Q", 1), ("Q", 2), ("Q", 3), ("Q", 4), ("R", 0, 1, 4), ("R", 1, 1, 4), ("R", 2, 1, 4),
    ("R", 3, -1, 4), ("P", 1), ("R", 4, -1, 4), ("P", 2), ("R", 0, 1, 3), ("R", 0, -1, 3), ("R", 1, 1, 3),
    ("R", 1, -1, 3), ("R", 2, 1, 3), ("R", 2, -1, 3), ("P", 3), ("X",), ("R", 0, 1, 2), ("R", 0, -1, 2),
    ("R", 1, 1, 2), ("R", 1, -1, 2), ("R", 3, 1, 3), ("R", 3, -1, 3), ("P", 4), ("R", 2, 1, 2), ("R", 0, -1, 1),
    ("R", 2, -1, 2), ("R", 0, 1, 1), ("R", 1, 1, 1), ("R", 1, -1, 1), ("R", 4, 1, 3), ("R", 4, -1, 3),
    ("R", 3, 1, 2), ("R", 3, -1, 2), ("R", 2, 1, 1), ("A", 0), ("R", 2, -1, 1), ("A", 1), ("R", 4, 1, 2),
    ("R", 4, -1, 2), ("R", 3, 1, 1), ("R", 3, -1, 1), ("N", 0, 1, 0), ("N", 0, -1, 0), ("N", 1, 1, 0),
    ("N", 1, -1, 0), ("A", 2), ("R", 4, 1, 1), ("R", 4, -1, 1), ("T", 3), ("T", 2), ("T", 1), ("A", 3),
    ("N", 0, 1, 1), ("N", 0, -1, 1), ("T", 0), ("N", 1, 1, 1), ("N", 1, -1, 1), ("W", 0, 3), ("N", 2, 1, 0),
    ("N", 2, -1, 0), ("A", 4), ("W", 1, 3), ("N", 0, 1, 2), ("N", 0, -1, 2), ("N", 1, 1, 2), ("N", 1, -1, 2),
    ("W", 0, 2), ("N", 3, -1, 0), ("N", 3, 1, 0), ("W", 1, 2), ("N", 4, 1, 0), ("N", 4, -1, 0), ("N", 2, 1, 1),
    ("N", 2, -1, 1), ("N", 0, -1, 3), ("W", 2, 3), ("N", 1, -1, 3), ("N", 0, 1, 3), ("N", 1, 1, 3), ("W", 0, 1),
    ("N", 3, -1, 1), ("N", 3, 1, 1), ("W", 1, 1), ("N", 4, -1, 1), ("W", 3, 3), ("N", 4, 1, 1), ("N", 2, -1, 2),
    ("N", 2, 1, 2), ("N", 0, 1, 4), ("W", 4, 3), ("N", 1, 1, 4), ("N", 3, -1, 2), ("W", 2, 2), ("W", 0, 0),
    ("N", 4, -1, 2), ("W", 1, 0), ("N", 3, 1, 2), ("N", 4, 1, 2), ("N", 2, -1, 3), ("W", 3, 2), ("W", 4, 2),
    ("N", 2, 1, 3), ("N", 3, -1, 3), ("N", 4, -1, 3), ("W", 2, 1), ("N", 3, 1, 3), ("N", 4, 1, 3), ("W", 3, 1),
    ("W", 4, 1), ("N", 3, -1, 4), ("N", 2, 1, 4), ("N", 4, -1, 4), ("W", 3, 0), ("W", 2, 0), ("W", 4, 0),
)


def encode(x):
    t = x * SCALE
    u = t * t
    return (u * t * jnp.abs(t)).astype(BF)


def decode(y):
    y = y.astype(F32)
    r = lax.rsqrt(lax.rsqrt(jnp.abs(y))) * (1.0 / SCALE)
    return jnp.where(y < 0.0, -r, r)


def kernel(tok_hbm, wg_hbm, wu_hbm, gh_hbm, hid_hbm, gg_hbm, gu_hbm, *scratch):
    n = len(CHUNKS)
    (tokt, tok, wg, wu, gh, hid, gg, gu, pk, pkr, pko, tk, tkt, part, frm), scratch = scratch[:15], scratch[15:]
    rs_send, rs_recv, act, g = (scratch[i * n : i * n + n] for i in range(4))
    (
        load_sem, out_sem, tok_send, tok_recv, oth_send, oth_recv, part_send, part_recv,
        rs_ssem, rs_rsem, swap_send, swap_recv, ag_send, ag_recv, fwd_send, fwd_recv,
    ) = scratch[4 * n :]
    row = lax.axis_index("row")
    col = lax.axis_index("col")
    dep = lax.axis_index("depth")
    z = col // 2
    core = col % 2
    other = 1 - core
    sent = []
    written = []

    def at(row_=None, z_=None, core_=None, dep_=None):
        return {
            "row": row if row_ is None else row_,
            "col": (z if z_ is None else z_) * 2 + (core if core_ is None else core_),
            "depth": dep if dep_ is None else dep_,
        }

    def along(step):
        return at(z_=lax.rem(z + step + 8, 8))

    def remote(src, dst, send, recv, device):
        return pltpu.make_async_remote_copy(
            src_ref=src, dst_ref=dst, send_sem=send, recv_sem=recv, device_id=device, device_id_type=MESH
        )

    def start(copy):
        copy.start()
        sent.append(copy)

    loads = [
        pltpu.make_async_copy(tok_hbm, tokt, load_sem.at[0]),
        pltpu.make_async_copy(wg_hbm, wg, load_sem.at[1]),
        pltpu.make_async_copy(wu_hbm, wu, load_sem.at[2]),
        pltpu.make_async_copy(gh_hbm.at[0], gh, load_sem.at[3]),
    ]
    for load in loads:
        load.start()

    barrier = pltpu.get_barrier_semaphore()
    peers = [at(row_=lax.rem(row + k, 8)) for k in range(1, 8)]
    beside = row + 1 - 2 * lax.rem(row, 2)
    across = at(row_=beside, dep_=1 - dep)
    peers += [across, at(dep_=1 - dep), along(1), along(-1), at(core_=other)]
    for peer in peers:
        pl.semaphore_signal(barrier, inc=1, device_id=peer, device_id_type=MESH)

    loads[0].wait()
    for m in range(6):
        tok[128 * m : 128 * m + 128, :] = tokt[:, 128 * m : 128 * m + 128].T
    for slot, offset in enumerate(OFFSETS):
        first = pl.multiple_of(lax.rem(z + offset + 8, 8) * 96, 32)
        low = tok[pl.ds(first, ROWS), :]
        high = tok[pl.ds(pl.multiple_of(first + ROWS, 16), ROWS), :]
        both = jnp.concatenate([low, high], axis=1)
        pk[slot] = both
        pkr[row, slot] = both
    pl.semaphore_wait(barrier, len(peers))

    def tok_copy(m, k, src):
        span = pl.ds(GROUPS[m][0], GROUPS[m][1] - GROUPS[m][0])
        return remote(pk.at[span], pkr.at[src, span], tok_send.at[m, k], tok_recv.at[m, src], at(row_=lax.rem(row + k, 8)))

    def cross_copy():
        return remote(pk, pko.at[row], oth_send.at[0], oth_recv.at[8], across)

    def oth_copy(k, src):
        return remote(pko.at[src], pko.at[src], oth_send.at[k], oth_recv.at[src], at(row_=lax.rem(row + k, 8)))

    def part_copy0(i):
        t0, w = CHUNKS[i]
        return remote(
            part.at[other, 0, :, :, t0 : t0 + w], frm.at[0, :, :, t0 : t0 + w],
            part_send.at[8 + i], part_recv.at[8 + i], at(core_=other),
        )

    def part_copy(slot):
        return remote(part.at[other, slot], frm.at[slot], part_send.at[slot], part_recv.at[slot], at(core_=other))

    def rs_copy(i, way, j):
        d = 0 if way == 1 else 1
        return remote(
            rs_send[i].at[d, j - 1], rs_recv[i].at[d, j - 1], rs_ssem.at[i, d, j - 1], rs_rsem.at[i, d, j - 1], along(way)
        )

    def swap_copy(i):
        return remote(act[i].at[1 - dep], g[i].at[14 + core, 1], swap_send.at[i], swap_recv.at[i], at(dep_=1 - dep))

    def ag_copy(i, way, hop):
        d = 0 if way == 1 else 1
        src = SLOT[-way * (hop - 1)]
        dst = SLOT[-way * hop] if hop < 4 else 0
        return remote(
            g[i].at[2 * src + core], g[i].at[2 * dst + core], ag_send.at[i, d, hop - 1], ag_recv.at[i, d, hop - 1], along(way)
        )

    def fwd_copy(i, slot, whose):
        block = g[i].at[2 * slot + whose]
        return remote(block, block, fwd_send.at[i, slot], fwd_recv.at[i, slot], at(core_=other))

    def unpack(packed, slot, which):
        for m in range(4):
            a = packed[2 * m, slot]
            b = packed[2 * m + 1, slot]
            for c in range(2):
                lanes = slice(64 * c, 64 * c + 64)
                tk[slot, c, which, :, 128 * m : 128 * m + 128] = jnp.concatenate([a[:, lanes], b[:, lanes]], axis=1)

    def project(slots, t0, w):
        lhs = jnp.concatenate([tk[slot, c, 0] for slot in slots for c in range(2)], axis=0)
        for q in range(4):
            first = HALF * (q % 2) + t0
            res = jnp.dot(lhs, (wg, wu)[q // 2][:, first : first + w], preferred_element_type=F32)
            for k, slot in enumerate(slots):
                for c in range(2):
                    rows = ROWS * (2 * k + c)
                    part[c, slot, q, :, t0 : t0 + w] = res[rows : rows + ROWS]

    arrived_parts = set()

    def need_part(slot, i):
        key = slot if slot else 8 + i
        if key not in arrived_parts:
            arrived_parts.add(key)
            (part_copy(slot) if slot else part_copy0(i)).wait_recv()

    def take_tokens(m):
        for k in range(1, 8):
            tok_copy(m, k, lax.rem(row + k, 8)).wait_recv()
        for slot in range(*GROUPS[m]):
            unpack(pkr, slot, 0)

    def step_q(i):
        if i == 0:
            take_tokens(0)
            loads[1].wait()
            loads[2].wait()
        project((0,), *CHUNKS[i])
        start(part_copy0(i))

    def step_p(m):
        take_tokens(m)
        slots = tuple(range(*GROUPS[m]))
        project(slots, 0, HALF)
        for slot in slots:
            start(part_copy(slot))

    def step_x():
        cross_copy().wait_recv()
        for k in range(1, 8):
            start(oth_copy(k, beside))

    unpacked = []

    def step_t(kg):
        if not unpacked:
            for k in range(1, 8):
                oth_copy(k, lax.rem(beside + k, 8)).wait_recv()
        unpacked.append(kg)
        for slot in (2 * kg, 2 * kg + 1):
            unpack(pko, slot, 1)
        rows = tk[2 * kg : 2 * kg + 2].reshape(384, 512)
        for m in range(3):
            tkt[:, 384 * kg + 128 * m : 384 * kg + 128 * m + 128] = rows[128 * m : 128 * m + 128, :].T

    def step_r(i, way, j):
        d = 0 if way == 1 else 1
        slot = SLOT[way * j] if j < 4 else 0
        t0, w = CHUNKS[i]
        arrived = j < HOPS[i][way]
        need_part(slot, i)
        if arrived:
            rs_copy(i, way, j + 1).wait_recv()

        @pl.loop(0, 12)
        def _(it):
            q = it // 3
            rows = pl.ds(pl.multiple_of(it % 3 * 16, 16), 16)
            x = part[core, slot, q, rows, t0 : t0 + w] + frm[slot, q, rows, t0 : t0 + w]
            if arrived:
                x = x + decode(rs_recv[i][d, j, q, rows, :])
            rs_send[i][d, j - 1, q, rows, :] = encode(x)

        start(rs_copy(i, way, j))

    def step_a(i):
        t0, w = CHUNKS[i]
        need_part(7, i)
        rs_copy(i, 1, 1).wait_recv()
        rs_copy(i, -1, 1).wait_recv()
        if loads[3] is not None:
            loads[3].wait()
            loads[3] = None

        def total(q, rows):
            x = part[core, 7, q, rows, t0 : t0 + w] + frm[7, q, rows, t0 : t0 + w]
            return x + decode(rs_recv[i][0, 0, q, rows, :]) + decode(rs_recv[i][1, 0, q, rows, :])

        @pl.loop(0, 3)
        def _(r):
            rows = pl.ds(pl.multiple_of(r * 16, 16), 16)
            for half in range(2):
                cols = slice(HALF * half + t0, HALF * half + t0 + w)
                gate = total(half, rows)
                up = total(2 + half, rows)
                squash = jax.nn.sigmoid(gate)
                hid[rows, cols] = (gate * squash * up).astype(BF)
                cot = gh[rows, cols].astype(F32)
                act[i][half, rows, 0:w] = (cot * up * squash * (1.0 + gate * (1.0 - squash))).astype(BF)
                act[i][half, rows, w : 2 * w] = (cot * gate * squash).astype(BF)

        start(swap_copy(i))
        g[i][14 + core, 0] = act[i][dep]

    begun = set()

    def step_n(i, way, hop):
        if hop == 0:
            if i not in begun:
                swap_copy(i).wait_recv()
        else:
            ag_copy(i, way, hop).wait_recv()
        if hop < HOPS[i][way]:
            start(ag_copy(i, way, hop + 1))
        if hop or i not in begun:
            start(fwd_copy(i, SLOT[-way * hop] if hop < 4 else 0, core))
        begun.add(i)

    summed = {}

    def step_w(i, kg):
        t0, w = CHUNKS[i]
        for slot in (2 * kg, 2 * kg + 1):
            fwd_copy(i, slot, other).wait_recv()
        first = i not in summed
        summed[i] = summed.get(i, 0) + 1

        @pl.loop(0, 2)
        def _(half):
            rows = pl.ds(pl.multiple_of(half * 256, 256), 256)
            lhs = tkt[rows, 384 * kg : 384 * kg + 384]
            for tile in range(0, 2 * w // 128, 2):
                rhs = g[i][4 * kg : 4 * kg + 4, :, :, 128 * tile : 128 * tile + 256].reshape(384, 256)
                res = jnp.dot(lhs, rhs, preferred_element_type=F32)
                for k in range(2):
                    out, c = (gg, tile + k) if tile + k < w // 128 else (gu, tile + k - w // 128)
                    cols = slice(t0 + 128 * c, t0 + 128 * c + 128)
                    piece = res[:, 128 * k : 128 * k + 128]
                    out[rows, cols] = piece if first else out[rows, cols] + piece

        if summed[i] == 4:
            for k, (src, dst) in enumerate(((gg, gg_hbm), (gu, gu_hbm))):
                copy = pltpu.make_async_copy(src.at[:, t0 : t0 + w], dst.at[:, t0 : t0 + w], out_sem.at[2 * i + k])
                copy.start()
                written.append(copy)

    for m in range(len(GROUPS)):
        for k in range(1, 8):
            start(tok_copy(m, k, row))
        if m == 1:
            start(cross_copy())
    steps = {"Q": step_q, "P": step_p, "X": step_x, "T": step_t, "R": step_r, "A": step_a, "N": step_n, "W": step_w}
    for name, *args in ORDER:
        steps[name](*args)
    out = pltpu.make_async_copy(hid, hid_hbm.at[0], out_sem.at[2 * n])
    out.start()
    for copy in sent:
        copy.wait_send()
    for copy in written:
        copy.wait()
    out.wait()


def hand_on(*refs):
    src, dst, buf, sems = refs[:3], refs[3:6], refs[6:9], refs[9]
    spans = [(0, slice(0, 1))] + [(k, pl.ds(128 * m, 128)) for m in range(4) for k in (1, 2)]
    reads = [pltpu.make_async_copy(src[k].at[s], buf[k].at[s], sems.at[0, m]) for m, (k, s) in enumerate(spans)]
    writes = [pltpu.make_async_copy(buf[k].at[s], dst[k].at[s], sems.at[1, m]) for m, (k, s) in enumerate(spans)]
    for read in reads:
        read.start()
    for read, write in zip(reads, writes):
        read.wait()
        write.start()
    for write in writes:
        write.wait()


def local(tokens, gate_weight, up_weight, grad_hidden):
    dma = pltpu.SemaphoreType.DMA
    v = pltpu.VMEM
    any_spec = pl.BlockSpec(memory_space=pl.ANY)
    n = len(CHUNKS)
    widths = [w for _, w in CHUNKS]
    out_shape = (
        jax.ShapeDtypeStruct((1, 48, 1792), BF),
        jax.ShapeDtypeStruct((512, 896), F32),
        jax.ShapeDtypeStruct((512, 896), F32),
    )
    outs = pl.pallas_call(
        kernel,
        out_shape=out_shape,
        in_specs=[any_spec] * 4,
        out_specs=(any_spec,) * 3,
        scratch_shapes=[
            v((64, 768), BF), v((768, 64), BF), v((512, 1792), BF), v((512, 1792), BF), v((48, 1792), BF),
            v((48, 1792), BF), v((512, 896), F32), v((512, 896), F32),
            v((8, 48, 128), BF), v((8, 8, 48, 128), BF), v((8, 8, 48, 128), BF),
            v((8, 2, 2, 48, 512), BF), v((512, 1536), BF),
            v((2, 8, 4, 48, 896), F32), v((8, 4, 48, 896), F32),
            *[v((2, 4, 4, 48, w), BF) for w in widths],
            *[v((2, 4, 4, 48, w), BF) for w in widths],
            *[v((2, 48, 2 * w), BF) for w in widths],
            *[v((16, 2, 48, 2 * w), BF) for w in widths],
            dma((4,)), dma((2 * n + 1,)), dma((5, 8)), dma((5, 8)), dma((8,)), dma((9,)), dma((8 + n,)), dma((8 + n,)),
            dma((n, 2, 4)), dma((n, 2, 4)), dma((n,)), dma((n,)), dma((n, 2, 4)), dma((n, 2, 4)), dma((n, 8)), dma((n, 8)),
        ],
        compiler_params=pltpu.CompilerParams(collective_id=0, has_side_effects=True, vmem_limit_bytes=60 << 20),
    )(tokens[0].T, gate_weight, up_weight, grad_hidden)
    return pl.pallas_call(
        hand_on,
        out_shape=out_shape,
        in_specs=[any_spec] * 3,
        out_specs=(any_spec,) * 3,
        scratch_shapes=[v(o.shape, o.dtype) for o in out_shape] + [dma((2, 9))],
    )(*outs)


def solution(mesh):
    in_specs = (
        P("depth", None, ("col", "row")),
        P("col", "row"),
        P("col", "row"),
        P("depth", "col", "row"),
    )
    out_specs = (P("depth", "col", "row"), P("col", ("row", "depth")), P("col", ("row", "depth")))
    return jax.shard_map(local, mesh=mesh, in_specs=in_specs, out_specs=out_specs, check_vma=False)
```

```python
import jax
import jax.numpy as jnp
from jax import lax
from jax.experimental import pallas as pl
from jax.experimental.pallas import tpu as pltpu
from jax.sharding import PartitionSpec as P

MESH = pl.DeviceIdType.MESH
BF = jnp.bfloat16
F32 = jnp.float32
OFFSETS = (4, 3, -3, 2, -2, 1, -1, 0)
SLOT = {offset: slot for slot, offset in enumerate(OFFSETS)}
GROUPS = ((0, 1), (1, 3), (3, 5), (5, 7), (7, 8))
ROWS = 48
HALF = 896
SCALE = 2.0**18
CHUNKS = ((0, 128), (128, 128), (256, 256), (512, 256), (768, 128))
HOPS = ({1: 4, -1: 3}, {1: 4, -1: 3}, {1: 4, -1: 3}, {1: 3, -1: 4}, {1: 3, -1: 4})

ORDER = (
    ("Q", 0), ("Q", 1), ("Q", 2), ("Q", 3), ("Q", 4), ("R", 0, 1, 4), ("R", 1, 1, 4), ("R", 2, 1, 4),
    ("R", 3, -1, 4), ("P", 1), ("R", 4, -1, 4), ("P", 2), ("R", 0, 1, 3), ("R", 0, -1, 3), ("R", 1, 1, 3),
    ("R", 1, -1, 3), ("R", 2, 1, 3), ("R", 2, -1, 3), ("P", 3), ("X",), ("R", 0, 1, 2), ("R", 0, -1, 2),
    ("R", 1, 1, 2), ("R", 1, -1, 2), ("R", 3, 1, 3), ("R", 3, -1, 3), ("P", 4), ("R", 2, 1, 2), ("R", 0, -1, 1),
    ("R", 2, -1, 2), ("R", 0, 1, 1), ("R", 1, 1, 1), ("R", 1, -1, 1), ("R", 4, 1, 3), ("R", 4, -1, 3),
    ("R", 3, 1, 2), ("R", 3, -1, 2), ("R", 2, 1, 1), ("A", 0), ("R", 2, -1, 1), ("A", 1), ("R", 4, 1, 2),
    ("R", 4, -1, 2), ("R", 3, 1, 1), ("R", 3, -1, 1), ("N", 0, 1, 0), ("N", 0, -1, 0), ("N", 1, 1, 0),
    ("N", 1, -1, 0), ("A", 2), ("R", 4, 1, 1), ("R", 4, -1, 1), ("T", 3), ("T", 2), ("T", 1), ("A", 3),
    ("N", 0, 1, 1), ("N", 0, -1, 1), ("T", 0), ("N", 1, 1, 1), ("N", 1, -1, 1), ("W", 0, 3), ("N", 2, 1, 0),
    ("N", 2, -1, 0), ("A", 4), ("W", 1, 3), ("N", 0, 1, 2), ("N", 0, -1, 2), ("N", 1, 1, 2), ("N", 1, -1, 2),
    ("W", 0, 2), ("N", 3, -1, 0), ("N", 3, 1, 0), ("W", 1, 2), ("N", 4, 1, 0), ("N", 4, -1, 0), ("N", 2, 1, 1),
    ("N", 2, -1, 1), ("N", 0, -1, 3), ("W", 2, 3), ("N", 1, -1, 3), ("N", 0, 1, 3), ("N", 1, 1, 3), ("W", 0, 1),
    ("N", 3, -1, 1), ("N", 3, 1, 1), ("W", 1, 1), ("N", 4, -1, 1), ("W", 3, 3), ("N", 4, 1, 1), ("N", 2, -1, 2),
    ("N", 2, 1, 2), ("N", 0, 1, 4), ("W", 4, 3), ("N", 1, 1, 4), ("N", 3, -1, 2), ("W", 2, 2), ("W", 0, 0),
    ("N", 4, -1, 2), ("W", 1, 0), ("N", 3, 1, 2), ("N", 4, 1, 2), ("N", 2, -1, 3), ("W", 3, 2), ("W", 4, 2),
    ("N", 2, 1, 3), ("N", 3, -1, 3), ("N", 4, -1, 3), ("W", 2, 1), ("N", 3, 1, 3), ("N", 4, 1, 3), ("W", 3, 1),
    ("W", 4, 1), ("N", 3, -1, 4), ("N", 2, 1, 4), ("N", 4, -1, 4), ("W", 3, 0), ("W", 2, 0), ("W", 4, 0),
)


def encode(x):
    t = x * SCALE
    u = t * t
    return (u * t * jnp.abs(t)).astype(BF)


def decode(y):
    y = y.astype(F32)
    r = lax.rsqrt(lax.rsqrt(jnp.abs(y))) * (1.0 / SCALE)
    return jnp.where(y < 0.0, -r, r)


def kernel(tok_hbm, wg_hbm, wu_hbm, gh_hbm, hid, gg, gu, *scratch):
    n = len(CHUNKS)
    (tokt, tok, wg, wu, gh, pk, pkr, pko, tk, tkt, part, frm), scratch = scratch[:12], scratch[12:]
    rs_send, rs_recv, act, g = (scratch[i * n : i * n + n] for i in range(4))
    (
        load_sem, tok_send, tok_recv, oth_send, oth_recv, part_send, part_recv,
        rs_ssem, rs_rsem, swap_send, swap_recv, ag_send, ag_recv, fwd_send, fwd_recv,
    ) = scratch[4 * n :]
    row = lax.axis_index("row")
    col = lax.axis_index("col")
    dep = lax.axis_index("depth")
    z = col // 2
    core = col % 2
    other = 1 - core
    sent = []

    def at(row_=None, z_=None, core_=None, dep_=None):
        return {
            "row": row if row_ is None else row_,
            "col": (z if z_ is None else z_) * 2 + (core if core_ is None else core_),
            "depth": dep if dep_ is None else dep_,
        }

    def along(step):
        return at(z_=lax.rem(z + step + 8, 8))

    def remote(src, dst, send, recv, device):
        return pltpu.make_async_remote_copy(
            src_ref=src, dst_ref=dst, send_sem=send, recv_sem=recv, device_id=device, device_id_type=MESH
        )

    def start(copy):
        copy.start()
        sent.append(copy)

    loads = [
        pltpu.make_async_copy(tok_hbm, tokt, load_sem.at[0]),
        pltpu.make_async_copy(wg_hbm, wg, load_sem.at[1]),
        pltpu.make_async_copy(wu_hbm, wu, load_sem.at[2]),
        pltpu.make_async_copy(gh_hbm.at[0], gh, load_sem.at[3]),
    ]
    for load in loads:
        load.start()

    barrier = pltpu.get_barrier_semaphore()
    peers = [at(row_=lax.rem(row + k, 8)) for k in range(1, 8)]
    beside = row + 1 - 2 * lax.rem(row, 2)
    across = at(row_=beside, dep_=1 - dep)
    peers += [across, at(dep_=1 - dep), along(1), along(-1), at(core_=other)]
    for peer in peers:
        pl.semaphore_signal(barrier, inc=1, device_id=peer, device_id_type=MESH)

    loads[0].wait()
    for m in range(6):
        tok[128 * m : 128 * m + 128, :] = tokt[:, 128 * m : 128 * m + 128].T
    for slot, offset in enumerate(OFFSETS):
        first = pl.multiple_of(lax.rem(z + offset + 8, 8) * 96, 32)
        low = tok[pl.ds(first, ROWS), :]
        high = tok[pl.ds(pl.multiple_of(first + ROWS, 16), ROWS), :]
        both = jnp.concatenate([low, high], axis=1)
        pk[slot] = both
        pkr[row, slot] = both
    pl.semaphore_wait(barrier, len(peers))

    def tok_copy(m, k, src):
        span = pl.ds(GROUPS[m][0], GROUPS[m][1] - GROUPS[m][0])
        return remote(pk.at[span], pkr.at[src, span], tok_send.at[m, k], tok_recv.at[m, src], at(row_=lax.rem(row + k, 8)))

    def cross_copy():
        return remote(pk, pko.at[row], oth_send.at[0], oth_recv.at[8], across)

    def oth_copy(k, src):
        return remote(pko.at[src], pko.at[src], oth_send.at[k], oth_recv.at[src], at(row_=lax.rem(row + k, 8)))

    def part_copy0(i):
        t0, w = CHUNKS[i]
        return remote(
            part.at[other, 0, :, :, t0 : t0 + w], frm.at[0, :, :, t0 : t0 + w],
            part_send.at[8 + i], part_recv.at[8 + i], at(core_=other),
        )

    def part_copy(slot):
        return remote(part.at[other, slot], frm.at[slot], part_send.at[slot], part_recv.at[slot], at(core_=other))

    def rs_copy(i, way, j):
        d = 0 if way == 1 else 1
        return remote(
            rs_send[i].at[d, j - 1], rs_recv[i].at[d, j - 1], rs_ssem.at[i, d, j - 1], rs_rsem.at[i, d, j - 1], along(way)
        )

    def swap_copy(i):
        return remote(act[i].at[1 - dep], g[i].at[14 + core, 1], swap_send.at[i], swap_recv.at[i], at(dep_=1 - dep))

    def ag_copy(i, way, hop):
        d = 0 if way == 1 else 1
        src = SLOT[-way * (hop - 1)]
        dst = SLOT[-way * hop] if hop < 4 else 0
        return remote(
            g[i].at[2 * src + core], g[i].at[2 * dst + core], ag_send.at[i, d, hop - 1], ag_recv.at[i, d, hop - 1], along(way)
        )

    def fwd_copy(i, slot, whose):
        block = g[i].at[2 * slot + whose]
        return remote(block, block, fwd_send.at[i, slot], fwd_recv.at[i, slot], at(core_=other))

    def unpack(packed, slot, which):
        for m in range(4):
            a = packed[2 * m, slot]
            b = packed[2 * m + 1, slot]
            for c in range(2):
                lanes = slice(64 * c, 64 * c + 64)
                tk[slot, c, which, :, 128 * m : 128 * m + 128] = jnp.concatenate([a[:, lanes], b[:, lanes]], axis=1)

    def project(slots, t0, w):
        lhs = jnp.concatenate([tk[slot, c, 0] for slot in slots for c in range(2)], axis=0)
        for q in range(4):
            first = HALF * (q % 2) + t0
            res = jnp.dot(lhs, (wg, wu)[q // 2][:, first : first + w], preferred_element_type=F32)
            for k, slot in enumerate(slots):
                for c in range(2):
                    rows = ROWS * (2 * k + c)
                    part[c, slot, q, :, t0 : t0 + w] = res[rows : rows + ROWS]

    arrived_parts = set()

    def need_part(slot, i):
        key = slot if slot else 8 + i
        if key not in arrived_parts:
            arrived_parts.add(key)
            (part_copy(slot) if slot else part_copy0(i)).wait_recv()

    def take_tokens(m):
        for k in range(1, 8):
            tok_copy(m, k, lax.rem(row + k, 8)).wait_recv()
        for slot in range(*GROUPS[m]):
            unpack(pkr, slot, 0)

    def step_q(i):
        if i == 0:
            take_tokens(0)
            loads[1].wait()
            loads[2].wait()
        project((0,), *CHUNKS[i])
        start(part_copy0(i))

    def step_p(m):
        take_tokens(m)
        slots = tuple(range(*GROUPS[m]))
        project(slots, 0, HALF)
        for slot in slots:
            start(part_copy(slot))

    def step_x():
        cross_copy().wait_recv()
        for k in range(1, 8):
            start(oth_copy(k, beside))

    unpacked = []

    def step_t(kg):
        if not unpacked:
            for k in range(1, 8):
                oth_copy(k, lax.rem(beside + k, 8)).wait_recv()
        unpacked.append(kg)
        for slot in (2 * kg, 2 * kg + 1):
            unpack(pko, slot, 1)
        rows = tk[2 * kg : 2 * kg + 2].reshape(384, 512)
        for m in range(3):
            tkt[:, 384 * kg + 128 * m : 384 * kg + 128 * m + 128] = rows[128 * m : 128 * m + 128, :].T

    def step_r(i, way, j):
        d = 0 if way == 1 else 1
        slot = SLOT[way * j] if j < 4 else 0
        t0, w = CHUNKS[i]
        arrived = j < HOPS[i][way]
        need_part(slot, i)
        if arrived:
            rs_copy(i, way, j + 1).wait_recv()

        @pl.loop(0, 12)
        def _(it):
            q = it // 3
            rows = pl.ds(pl.multiple_of(it % 3 * 16, 16), 16)
            x = part[core, slot, q, rows, t0 : t0 + w] + frm[slot, q, rows, t0 : t0 + w]
            if arrived:
                x = x + decode(rs_recv[i][d, j, q, rows, :])
            rs_send[i][d, j - 1, q, rows, :] = encode(x)

        start(rs_copy(i, way, j))

    def step_a(i):
        t0, w = CHUNKS[i]
        need_part(7, i)
        rs_copy(i, 1, 1).wait_recv()
        rs_copy(i, -1, 1).wait_recv()
        if loads[3] is not None:
            loads[3].wait()
            loads[3] = None

        def total(q, rows):
            x = part[core, 7, q, rows, t0 : t0 + w] + frm[7, q, rows, t0 : t0 + w]
            return x + decode(rs_recv[i][0, 0, q, rows, :]) + decode(rs_recv[i][1, 0, q, rows, :])

        @pl.loop(0, 3)
        def _(r):
            rows = pl.ds(pl.multiple_of(r * 16, 16), 16)
            for half in range(2):
                cols = slice(HALF * half + t0, HALF * half + t0 + w)
                gate = total(half, rows)
                up = total(2 + half, rows)
                squash = jax.nn.sigmoid(gate)
                hid[0, rows, cols] = (gate * squash * up).astype(BF)
                cot = gh[rows, cols].astype(F32)
                act[i][half, rows, 0:w] = (cot * up * squash * (1.0 + gate * (1.0 - squash))).astype(BF)
                act[i][half, rows, w : 2 * w] = (cot * gate * squash).astype(BF)

        start(swap_copy(i))
        g[i][14 + core, 0] = act[i][dep]

    begun = set()

    def step_n(i, way, hop):
        if hop == 0:
            if i not in begun:
                swap_copy(i).wait_recv()
        else:
            ag_copy(i, way, hop).wait_recv()
        if hop < HOPS[i][way]:
            start(ag_copy(i, way, hop + 1))
        if hop or i not in begun:
            start(fwd_copy(i, SLOT[-way * hop] if hop < 4 else 0, core))
        begun.add(i)

    summed = {}

    def step_w(i, kg):
        t0, w = CHUNKS[i]
        for slot in (2 * kg, 2 * kg + 1):
            fwd_copy(i, slot, other).wait_recv()
        first = i not in summed
        summed[i] = summed.get(i, 0) + 1

        @pl.loop(0, 2)
        def _(half):
            rows = pl.ds(pl.multiple_of(half * 256, 256), 256)
            lhs = tkt[rows, 384 * kg : 384 * kg + 384]
            for tile in range(0, 2 * w // 128, 2):
                rhs = g[i][4 * kg : 4 * kg + 4, :, :, 128 * tile : 128 * tile + 256].reshape(384, 256)
                res = jnp.dot(lhs, rhs, preferred_element_type=F32)
                for k in range(2):
                    out, c = (gg, tile + k) if tile + k < w // 128 else (gu, tile + k - w // 128)
                    cols = slice(t0 + 128 * c, t0 + 128 * c + 128)
                    piece = res[:, 128 * k : 128 * k + 128]
                    out[rows, cols] = piece if first else out[rows, cols] + piece

    for m in range(len(GROUPS)):
        for k in range(1, 8):
            start(tok_copy(m, k, row))
        if m == 1:
            start(cross_copy())
    steps = {"Q": step_q, "P": step_p, "X": step_x, "T": step_t, "R": step_r, "A": step_a, "N": step_n, "W": step_w}
    for name, *args in ORDER:
        steps[name](*args)
    for copy in sent:
        copy.wait_send()


def hand_on(*refs):
    src, dst, sems = refs[:3], refs[3:6], refs[6]
    copies = [pltpu.make_async_copy(src[k], dst[k], sems.at[k]) for k in range(3)]
    for copy in copies:
        copy.start()
    for copy in copies:
        copy.wait()


def local(tokens, gate_weight, up_weight, grad_hidden):
    dma = pltpu.SemaphoreType.DMA
    v = pltpu.VMEM
    any_spec = pl.BlockSpec(memory_space=pl.ANY)
    n = len(CHUNKS)
    widths = [w for _, w in CHUNKS]
    out_shape = (
        jax.ShapeDtypeStruct((1, 48, 1792), BF),
        jax.ShapeDtypeStruct((512, 896), F32),
        jax.ShapeDtypeStruct((512, 896), F32),
    )
    outs = pl.pallas_call(
        kernel,
        out_shape=out_shape,
        in_specs=[pl.BlockSpec(memory_space=pltpu.HBM)] * 4,
        out_specs=(pl.BlockSpec(memory_space=v),) * 3,
        scratch_shapes=[
            v((64, 768), BF), v((768, 64), BF), v((512, 1792), BF), v((512, 1792), BF), v((48, 1792), BF),
            v((8, 48, 128), BF), v((8, 8, 48, 128), BF), v((8, 8, 48, 128), BF),
            v((8, 2, 2, 48, 512), BF), v((512, 1536), BF),
            v((2, 8, 4, 48, 896), F32), v((8, 4, 48, 896), F32),
            *[v((2, 4, 4, 48, w), BF) for w in widths],
            *[v((2, 4, 4, 48, w), BF) for w in widths],
            *[v((2, 48, 2 * w), BF) for w in widths],
            *[v((16, 2, 48, 2 * w), BF) for w in widths],
            dma((4,)), dma((5, 8)), dma((5, 8)), dma((8,)), dma((9,)), dma((8 + n,)), dma((8 + n,)),
            dma((n, 2, 4)), dma((n, 2, 4)), dma((n,)), dma((n,)), dma((n, 2, 4)), dma((n, 2, 4)), dma((n, 8)), dma((n, 8)),
        ],
        compiler_params=pltpu.CompilerParams(collective_id=0, has_side_effects=True, vmem_limit_bytes=46 << 20),
    )(*(pltpu.with_memory_space_constraint(a, pltpu.HBM) for a in (tokens[0].T, gate_weight, up_weight, grad_hidden)))
    return pl.pallas_call(
        hand_on,
        out_shape=out_shape,
        in_specs=[pl.BlockSpec(memory_space=v)] * 3,
        out_specs=(any_spec,) * 3,
        scratch_shapes=[dma((3,))],
        compiler_params=pltpu.CompilerParams(vmem_limit_bytes=8 << 20),
    )(*outs)


def solution(mesh):
    in_specs = (
        P("depth", None, ("col", "row")),
        P("col", "row"),
        P("col", "row"),
        P("depth", "col", "row"),
    )
    out_specs = (P("depth", "col", "row"), P("col", ("row", "depth")), P("col", ("row", "depth")))
    return jax.shard_map(local, mesh=mesh, in_specs=in_specs, out_specs=out_specs, check_vma=False)
```

```python
import jax
import jax.numpy as jnp
from jax import lax
from jax.experimental import pallas as pl
from jax.experimental.pallas import tpu as pltpu
from jax.sharding import PartitionSpec as P

MESH = pl.DeviceIdType.MESH
BF = jnp.bfloat16
F32 = jnp.float32
OFFSETS = (4, 3, -3, 2, -2, 1, -1, 0)
SLOT = {offset: slot for slot, offset in enumerate(OFFSETS)}
GROUPS = ((0, 1), (1, 3), (3, 5), (5, 7), (7, 8))
ROWS = 48
HALF = 896
SCALE = 2.0**18
CHUNKS = ((0, 128), (128, 128), (256, 128), (384, 256), (640, 128), (768, 128))
HOPS = ({1: 4, -1: 3}, {1: 3, -1: 4}, {1: 3, -1: 4}, {1: 3, -1: 4}, {1: 4, -1: 3}, {1: 4, -1: 3})

ORDER = (
    ("Q", 0), ("Q", 1), ("Q", 2), ("Q", 3), ("R", 0, 1, 4), ("R", 1, -1, 4), ("R", 2, -1, 4), ("Q", 4),
    ("R", 3, -1, 4), ("Q", 5), ("P", 1), ("R", 4, 1, 4), ("R", 5, 1, 4), ("P", 2), ("R", 0, 1, 3), ("R", 0, -1, 3),
    ("R", 1, 1, 3), ("R", 1, -1, 3), ("R", 2, 1, 3), ("R", 2, -1, 3), ("R", 3, 1, 3), ("R", 3, -1, 3), ("P", 3),
    ("X",), ("R", 0, 1, 2), ("R", 0, -1, 2), ("R", 1, 1, 2), ("R", 1, -1, 2), ("R", 2, 1, 2), ("R", 2, -1, 2),
    ("R", 4, 1, 3), ("R", 4, -1, 3), ("P", 4), ("R", 0, 1, 1), ("R", 0, -1, 1), ("R", 3, 1, 2), ("R", 3, -1, 2),
    ("R", 1, 1, 1), ("R", 1, -1, 1), ("R", 2, 1, 1), ("R", 2, -1, 1), ("R", 4, 1, 2), ("R", 4, -1, 2), ("A", 0),
    ("R", 5, 1, 3), ("R", 5, -1, 3), ("R", 3, 1, 1), ("R", 3, -1, 1), ("A", 1), ("A", 2), ("N", 0, 1, 0),
    ("N", 0, -1, 0), ("R", 4, 1, 1), ("R", 4, -1, 1), ("R", 5, 1, 2), ("R", 5, -1, 2), ("N", 1, 1, 0),
    ("N", 1, -1, 0), ("A", 3), ("N", 2, 1, 0), ("N", 0, 1, 1), ("N", 2, -1, 0), ("N", 0, -1, 1), ("T", 3), ("T", 2),
    ("A", 4), ("R", 5, 1, 1), ("R", 5, -1, 1), ("T", 1), ("N", 1, 1, 1), ("N", 1, -1, 1), ("T", 0), ("N", 2, 1, 1),
    ("W", 0, 3), ("N", 2, -1, 1), ("W", 1, 3), ("N", 0, 1, 2), ("N", 3, 1, 0), ("N", 3, -1, 0), ("W", 2, 3),
    ("N", 0, -1, 2), ("A", 5), ("W", 0, 2), ("N", 1, 1, 2), ("N", 4, -1, 0), ("N", 4, 1, 0), ("N", 1, -1, 2),
    ("W", 1, 2), ("N", 2, 1, 2), ("N", 2, -1, 2), ("N", 0, 1, 3), ("W", 2, 2), ("N", 3, -1, 1), ("N", 5, 1, 0),
    ("W", 0, 1), ("N", 0, -1, 3), ("N", 3, 1, 1), ("N", 1, 1, 3), ("N", 5, -1, 0), ("N", 4, -1, 1), ("W", 3, 3),
    ("W", 1, 1), ("N", 2, 1, 3), ("N", 1, -1, 3), ("N", 4, 1, 1), ("N", 0, 1, 4), ("N", 2, -1, 3), ("W", 2, 1),
    ("W", 4, 3), ("N", 5, 1, 1), ("N", 3, -1, 2), ("W", 0, 0), ("W", 5, 3), ("N", 3, 1, 2), ("N", 5, -1, 1),
    ("N", 4, 1, 2), ("N", 4, -1, 2), ("N", 1, -1, 4), ("W", 3, 2), ("N", 5, 1, 2), ("N", 2, -1, 4), ("W", 4, 2),
    ("W", 1, 0), ("W", 5, 2), ("W", 2, 0), ("N", 3, -1, 3), ("N", 3, 1, 3), ("N", 5, -1, 2), ("N", 4, 1, 3),
    ("W", 3, 1), ("N", 4, -1, 3), ("N", 5, 1, 3), ("W", 4, 1), ("W", 5, 1), ("N", 3, -1, 4), ("N", 4, 1, 4),
    ("N", 5, -1, 3), ("N", 5, 1, 4), ("W", 3, 0), ("W", 4, 0), ("W", 5, 0),
)


def encode(x):
    t = x * SCALE
    u = t * t
    return (u * t * jnp.abs(t)).astype(BF)


def decode(y):
    y = y.astype(F32)
    r = lax.rsqrt(lax.rsqrt(jnp.abs(y))) * (1.0 / SCALE)
    return jnp.where(y < 0.0, -r, r)


def kernel(tok_hbm, wg_hbm, wu_hbm, gh_hbm, hid, gg, gu, *scratch):
    n = len(CHUNKS)
    (tokt, tok, wg, wu, gh, pk, pkr, pko, tk, tkt, part, frm), scratch = scratch[:12], scratch[12:]
    rs_send, rs_recv, act, g = (scratch[i * n : i * n + n] for i in range(4))
    (
        load_sem, tok_send, tok_recv, oth_send, oth_recv, part_send, part_recv,
        rs_ssem, rs_rsem, swap_send, swap_recv, ag_send, ag_recv, fwd_send, fwd_recv,
    ) = scratch[4 * n :]
    row = lax.axis_index("row")
    col = lax.axis_index("col")
    dep = lax.axis_index("depth")
    z = col // 2
    core = col % 2
    other = 1 - core
    sent = []

    def at(row_=None, z_=None, core_=None, dep_=None):
        return {
            "row": row if row_ is None else row_,
            "col": (z if z_ is None else z_) * 2 + (core if core_ is None else core_),
            "depth": dep if dep_ is None else dep_,
        }

    def along(step):
        return at(z_=lax.rem(z + step + 8, 8))

    def remote(src, dst, send, recv, device):
        return pltpu.make_async_remote_copy(
            src_ref=src, dst_ref=dst, send_sem=send, recv_sem=recv, device_id=device, device_id_type=MESH
        )

    def start(copy):
        copy.start()
        sent.append(copy)

    loads = [
        pltpu.make_async_copy(tok_hbm, tokt, load_sem.at[0]),
        pltpu.make_async_copy(wg_hbm, wg, load_sem.at[1]),
        pltpu.make_async_copy(wu_hbm, wu, load_sem.at[2]),
        pltpu.make_async_copy(gh_hbm.at[0], gh, load_sem.at[3]),
    ]
    for load in loads:
        load.start()

    barrier = pltpu.get_barrier_semaphore()
    peers = [at(row_=lax.rem(row + k, 8)) for k in range(1, 8)]
    beside = row + 1 - 2 * lax.rem(row, 2)
    across = at(row_=beside, dep_=1 - dep)
    peers += [across, at(dep_=1 - dep), along(1), along(-1), at(core_=other)]
    for peer in peers:
        pl.semaphore_signal(barrier, inc=1, device_id=peer, device_id_type=MESH)

    loads[0].wait()
    for m in range(6):
        tok[128 * m : 128 * m + 128, :] = tokt[:, 128 * m : 128 * m + 128].T

    def pack(slot):
        first = pl.multiple_of(lax.rem(z + OFFSETS[slot] + 8, 8) * 96, 32)
        low = tok[pl.ds(first, ROWS), :]
        high = tok[pl.ds(pl.multiple_of(first + ROWS, 16), ROWS), :]
        both = jnp.concatenate([low, high], axis=1)
        pk[slot] = both
        pkr[row, slot] = both

    def tok_copy(m, k, src):
        span = pl.ds(GROUPS[m][0], GROUPS[m][1] - GROUPS[m][0])
        return remote(pk.at[span], pkr.at[src, span], tok_send.at[m, k], tok_recv.at[m, src], at(row_=lax.rem(row + k, 8)))

    def cross_copy():
        return remote(pk, pko.at[row], oth_send.at[0], oth_recv.at[8], across)

    def oth_copy(k, src):
        return remote(pko.at[src], pko.at[src], oth_send.at[k], oth_recv.at[src], at(row_=lax.rem(row + k, 8)))

    def part_copy0(i):
        t0, w = CHUNKS[i]
        return remote(
            part.at[other, 0, :, :, t0 : t0 + w], frm.at[0, :, :, t0 : t0 + w],
            part_send.at[8 + i], part_recv.at[8 + i], at(core_=other),
        )

    def part_copy(slot):
        return remote(part.at[other, slot], frm.at[slot], part_send.at[slot], part_recv.at[slot], at(core_=other))

    def rs_copy(i, way, j):
        d = 0 if way == 1 else 1
        return remote(
            rs_send[i].at[d, j - 1], rs_recv[i].at[d, j - 1], rs_ssem.at[i, d, j - 1], rs_rsem.at[i, d, j - 1], along(way)
        )

    def swap_copy(i):
        return remote(act[i].at[1 - dep], g[i].at[14 + core, 1], swap_send.at[i], swap_recv.at[i], at(dep_=1 - dep))

    def ag_copy(i, way, hop):
        d = 0 if way == 1 else 1
        src = SLOT[-way * (hop - 1)]
        dst = SLOT[-way * hop] if hop < 4 else 0
        return remote(
            g[i].at[2 * src + core], g[i].at[2 * dst + core], ag_send.at[i, d, hop - 1], ag_recv.at[i, d, hop - 1], along(way)
        )

    def fwd_copy(i, slot, whose):
        block = g[i].at[2 * slot + whose]
        return remote(block, block, fwd_send.at[i, slot], fwd_recv.at[i, slot], at(core_=other))

    def unpack(packed, slot, which):
        for m in range(4):
            a = packed[2 * m, slot]
            b = packed[2 * m + 1, slot]
            for c in range(2):
                lanes = slice(64 * c, 64 * c + 64)
                tk[slot, c, which, :, 128 * m : 128 * m + 128] = jnp.concatenate([a[:, lanes], b[:, lanes]], axis=1)

    def project(slots, t0, w):
        lhs = jnp.concatenate([tk[slot, c, 0] for slot in slots for c in range(2)], axis=0)
        for q in range(4):
            first = HALF * (q % 2) + t0
            res = jnp.dot(lhs, (wg, wu)[q // 2][:, first : first + w], preferred_element_type=F32)
            for k, slot in enumerate(slots):
                for c in range(2):
                    rows = ROWS * (2 * k + c)
                    part[c, slot, q, :, t0 : t0 + w] = res[rows : rows + ROWS]

    arrived_parts = set()

    def need_part(slot, i):
        key = slot if slot else 8 + i
        if key not in arrived_parts:
            arrived_parts.add(key)
            (part_copy(slot) if slot else part_copy0(i)).wait_recv()

    def take_tokens(m):
        for k in range(1, 8):
            tok_copy(m, k, lax.rem(row + k, 8)).wait_recv()
        for slot in range(*GROUPS[m]):
            unpack(pkr, slot, 0)

    def step_q(i):
        if i == 0:
            take_tokens(0)
            loads[1].wait()
            loads[2].wait()
        project((0,), *CHUNKS[i])
        start(part_copy0(i))

    def step_p(m):
        take_tokens(m)
        slots = tuple(range(*GROUPS[m]))
        project(slots, 0, HALF)
        for slot in slots:
            start(part_copy(slot))

    def step_x():
        cross_copy().wait_recv()
        for k in range(1, 8):
            start(oth_copy(k, beside))

    unpacked = []

    def step_t(kg):
        if not unpacked:
            for k in range(1, 8):
                oth_copy(k, lax.rem(beside + k, 8)).wait_recv()
        unpacked.append(kg)
        for slot in (2 * kg, 2 * kg + 1):
            unpack(pko, slot, 1)
        rows = tk[2 * kg : 2 * kg + 2].reshape(384, 512)
        for m in range(3):
            tkt[:, 384 * kg + 128 * m : 384 * kg + 128 * m + 128] = rows[128 * m : 128 * m + 128, :].T

    def step_r(i, way, j):
        d = 0 if way == 1 else 1
        slot = SLOT[way * j] if j < 4 else 0
        t0, w = CHUNKS[i]
        arrived = j < HOPS[i][way]
        need_part(slot, i)
        if arrived:
            rs_copy(i, way, j + 1).wait_recv()

        @pl.loop(0, 12)
        def _(it):
            q = it // 3
            rows = pl.ds(pl.multiple_of(it % 3 * 16, 16), 16)
            x = part[core, slot, q, rows, t0 : t0 + w] + frm[slot, q, rows, t0 : t0 + w]
            if arrived:
                x = x + decode(rs_recv[i][d, j, q, rows, :])
            rs_send[i][d, j - 1, q, rows, :] = encode(x)

        start(rs_copy(i, way, j))

    def step_a(i):
        t0, w = CHUNKS[i]
        need_part(7, i)
        rs_copy(i, 1, 1).wait_recv()
        rs_copy(i, -1, 1).wait_recv()
        if loads[3] is not None:
            loads[3].wait()
            loads[3] = None

        def total(q, rows):
            x = part[core, 7, q, rows, t0 : t0 + w] + frm[7, q, rows, t0 : t0 + w]
            return x + decode(rs_recv[i][0, 0, q, rows, :]) + decode(rs_recv[i][1, 0, q, rows, :])

        @pl.loop(0, 3)
        def _(r):
            rows = pl.ds(pl.multiple_of(r * 16, 16), 16)
            for half in range(2):
                cols = slice(HALF * half + t0, HALF * half + t0 + w)
                gate = total(half, rows)
                up = total(2 + half, rows)
                squash = jax.nn.sigmoid(gate)
                hid[0, rows, cols] = (gate * squash * up).astype(BF)
                cot = gh[rows, cols].astype(F32)
                act[i][half, rows, 0:w] = (cot * up * squash * (1.0 + gate * (1.0 - squash))).astype(BF)
                act[i][half, rows, w : 2 * w] = (cot * gate * squash).astype(BF)

        start(swap_copy(i))
        g[i][14 + core, 0] = act[i][dep]

    begun = set()

    def step_n(i, way, hop):
        if hop == 0:
            if i not in begun:
                swap_copy(i).wait_recv()
        else:
            ag_copy(i, way, hop).wait_recv()
        if hop < HOPS[i][way]:
            start(ag_copy(i, way, hop + 1))
        if hop or i not in begun:
            start(fwd_copy(i, SLOT[-way * hop] if hop < 4 else 0, core))
        begun.add(i)

    summed = {}

    def step_w(i, kg):
        t0, w = CHUNKS[i]
        for slot in (2 * kg, 2 * kg + 1):
            fwd_copy(i, slot, other).wait_recv()
        first = i not in summed
        summed[i] = summed.get(i, 0) + 1

        @pl.loop(0, 2)
        def _(half):
            rows = pl.ds(pl.multiple_of(half * 256, 256), 256)
            lhs = tkt[rows, 384 * kg : 384 * kg + 384]
            for tile in range(0, 2 * w // 128, 2):
                rhs = g[i][4 * kg : 4 * kg + 4, :, :, 128 * tile : 128 * tile + 256].reshape(384, 256)
                res = jnp.dot(lhs, rhs, preferred_element_type=F32)
                for k in range(2):
                    out, c = (gg, tile + k) if tile + k < w // 128 else (gu, tile + k - w // 128)
                    cols = slice(t0 + 128 * c, t0 + 128 * c + 128)
                    piece = res[:, 128 * k : 128 * k + 128]
                    out[rows, cols] = piece if first else out[rows, cols] + piece

    for m in range(len(GROUPS)):
        for slot in range(*GROUPS[m]):
            pack(slot)
        if m == 0:
            pl.semaphore_wait(barrier, len(peers))
        for k in range(1, 8):
            start(tok_copy(m, k, row))
    start(cross_copy())
    steps = {"Q": step_q, "P": step_p, "X": step_x, "T": step_t, "R": step_r, "A": step_a, "N": step_n, "W": step_w}
    for name, *args in ORDER:
        steps[name](*args)
    for copy in sent:
        copy.wait_send()


def hand_on(*refs):
    src, dst, sems = refs[:3], refs[3:6], refs[6]
    copies = [pltpu.make_async_copy(src[k], dst[k], sems.at[k]) for k in range(3)]
    for copy in copies:
        copy.start()
    for copy in copies:
        copy.wait()


def local(tokens, gate_weight, up_weight, grad_hidden):
    dma = pltpu.SemaphoreType.DMA
    v = pltpu.VMEM
    any_spec = pl.BlockSpec(memory_space=pl.ANY)
    n = len(CHUNKS)
    widths = [w for _, w in CHUNKS]
    out_shape = (
        jax.ShapeDtypeStruct((1, 48, 1792), BF),
        jax.ShapeDtypeStruct((512, 896), F32),
        jax.ShapeDtypeStruct((512, 896), F32),
    )
    outs = pl.pallas_call(
        kernel,
        out_shape=out_shape,
        in_specs=[pl.BlockSpec(memory_space=pltpu.HBM)] * 4,
        out_specs=(pl.BlockSpec(memory_space=v),) * 3,
        scratch_shapes=[
            v((64, 768), BF), v((768, 64), BF), v((512, 1792), BF), v((512, 1792), BF), v((48, 1792), BF),
            v((8, 48, 128), BF), v((8, 8, 48, 128), BF), v((8, 8, 48, 128), BF),
            v((8, 2, 2, 48, 512), BF), v((512, 1536), BF),
            v((2, 8, 4, 48, 896), F32), v((8, 4, 48, 896), F32),
            *[v((2, 4, 4, 48, w), BF) for w in widths],
            *[v((2, 4, 4, 48, w), BF) for w in widths],
            *[v((2, 48, 2 * w), BF) for w in widths],
            *[v((16, 2, 48, 2 * w), BF) for w in widths],
            dma((4,)), dma((5, 8)), dma((5, 8)), dma((8,)), dma((9,)), dma((8 + n,)), dma((8 + n,)),
            dma((n, 2, 4)), dma((n, 2, 4)), dma((n,)), dma((n,)), dma((n, 2, 4)), dma((n, 2, 4)), dma((n, 8)), dma((n, 8)),
        ],
        compiler_params=pltpu.CompilerParams(collective_id=0, has_side_effects=True, vmem_limit_bytes=46 << 20),
    )(*(pltpu.with_memory_space_constraint(a, pltpu.HBM) for a in (tokens[0].T, gate_weight, up_weight, grad_hidden)))
    return pl.pallas_call(
        hand_on,
        out_shape=out_shape,
        in_specs=[pl.BlockSpec(memory_space=v)] * 3,
        out_specs=(any_spec,) * 3,
        scratch_shapes=[dma((3,))],
        compiler_params=pltpu.CompilerParams(vmem_limit_bytes=8 << 20),
    )(*outs)


def solution(mesh):
    in_specs = (
        P("depth", None, ("col", "row")),
        P("col", "row"),
        P("col", "row"),
        P("depth", "col", "row"),
    )
    out_specs = (P("depth", "col", "row"), P("col", ("row", "depth")), P("col", ("row", "depth")))
    return jax.shard_map(local, mesh=mesh, in_specs=in_specs, out_specs=out_specs, check_vma=False)
```

```python
import jax
import jax.numpy as jnp
from jax import lax
from jax.experimental import pallas as pl
from jax.experimental.pallas import tpu as pltpu
from jax.sharding import PartitionSpec as P

MESH = pl.DeviceIdType.MESH
BF = jnp.bfloat16
F32 = jnp.float32
OFFSETS = (4, 3, -3, 2, -2, 1, -1, 0)
SLOT = {offset: slot for slot, offset in enumerate(OFFSETS)}
GROUPS = ((0, 1), (1, 3), (3, 5), (5, 7), (7, 8))
ROWS = 48
HALF = 896
SCALE = 2.0**18
CHUNKS = ((0, 128), (128, 128), (256, 256), (512, 256), (768, 128))
HOPS = ({1: 4, -1: 3}, {1: 4, -1: 3}, {1: 4, -1: 3}, {1: 3, -1: 4}, {1: 3, -1: 4})

ORDER = (
    ("Q", 0), ("Q", 1), ("Q", 2), ("R", 0, 1, 4), ("Q", 3), ("R", 1, 1, 4), ("R", 2, 1, 4), ("Q", 4),
    ("R", 3, -1, 4), ("P", 1), ("R", 4, -1, 4), ("P", 2), ("R", 0, 1, 3), ("R", 0, -1, 3), ("R", 1, 1, 3),
    ("R", 1, -1, 3), ("R", 2, 1, 3), ("R", 2, -1, 3), ("P", 3), ("X",), ("R", 0, 1, 2), ("R", 0, -1, 2),
    ("R", 1, 1, 2), ("R", 1, -1, 2), ("R", 3, 1, 3), ("R", 3, -1, 3), ("P", 4), ("R", 2, 1, 2), ("R", 0, -1, 1),
    ("R", 2, -1, 2), ("R", 0, 1, 1), ("R", 1, 1, 1), ("R", 1, -1, 1), ("R", 4, 1, 3), ("R", 4, -1, 3),
    ("R", 3, 1, 2), ("R", 3, -1, 2), ("R", 2, 1, 1), ("A", 0), ("R", 2, -1, 1), ("A", 1), ("R", 4, 1, 2),
    ("R", 4, -1, 2), ("R", 3, 1, 1), ("R", 3, -1, 1), ("N", 0, 1, 0), ("N", 0, -1, 0), ("N", 1, 1, 0),
    ("N", 1, -1, 0), ("A", 2), ("R", 4, 1, 1), ("R", 4, -1, 1), ("T", 3), ("T", 2), ("T", 1), ("A", 3),
    ("N", 0, 1, 1), ("N", 0, -1, 1), ("T", 0), ("N", 1, 1, 1), ("N", 1, -1, 1), ("W", 0, 3), ("N", 2, 1, 0),
    ("N", 2, -1, 0), ("A", 4), ("W", 1, 3), ("N", 0, 1, 2), ("N", 0, -1, 2), ("N", 1, 1, 2), ("N", 1, -1, 2),
    ("W", 0, 2), ("N", 3, 1, 0), ("N", 3, -1, 0), ("W", 1, 2), ("N", 4, 1, 0), ("N", 4, -1, 0), ("N", 2, 1, 1),
    ("N", 2, -1, 1), ("N", 0, -1, 3), ("W", 2, 3), ("N", 1, -1, 3), ("N", 0, 1, 3), ("N", 1, 1, 3), ("W", 0, 1),
    ("N", 3, -1, 1), ("N", 3, 1, 1), ("W", 1, 1), ("N", 4, -1, 1), ("W", 3, 3), ("N", 4, 1, 1), ("N", 2, -1, 2),
    ("N", 2, 1, 2), ("N", 0, 1, 4), ("W", 4, 3), ("N", 1, 1, 4), ("N", 3, -1, 2), ("W", 2, 2), ("W", 0, 0),
    ("N", 4, -1, 2), ("W", 1, 0), ("N", 3, 1, 2), ("N", 4, 1, 2), ("N", 2, -1, 3), ("W", 3, 2), ("W", 4, 2),
    ("N", 2, 1, 3), ("N", 3, -1, 3), ("N", 4, -1, 3), ("W", 2, 1), ("N", 3, 1, 3), ("N", 4, 1, 3), ("W", 3, 1),
    ("W", 4, 1), ("N", 3, -1, 4), ("N", 2, 1, 4), ("N", 4, -1, 4), ("W", 3, 0), ("W", 2, 0), ("W", 4, 0),
)


def encode(x):
    t = x * SCALE
    u = t * t
    return (u * t * jnp.abs(t)).astype(BF)


def decode(y):
    y = y.astype(F32)
    r = lax.rsqrt(lax.rsqrt(jnp.abs(y))) * (1.0 / SCALE)
    return jnp.where(y < 0.0, -r, r)


def kernel(tok_hbm, wg_hbm, wu_hbm, gh_hbm, hid, gg, gu, *scratch):
    n = len(CHUNKS)
    (tokt, tok, wg, wu, gh, pk, pkr, pko, tk, tkt, part, frm), scratch = scratch[:12], scratch[12:]
    rs_send, rs_recv, act, g = (scratch[i * n : i * n + n] for i in range(4))
    (
        load_sem, tok_send, tok_recv, oth_send, oth_recv, part_send, part_recv,
        rs_ssem, rs_rsem, swap_send, swap_recv, ag_send, ag_recv, fwd_send, fwd_recv,
    ) = scratch[4 * n :]
    row = lax.axis_index("row")
    col = lax.axis_index("col")
    dep = lax.axis_index("depth")
    z = col // 2
    core = col % 2
    other = 1 - core
    sent = []

    def at(row_=None, z_=None, core_=None, dep_=None):
        return {
            "row": row if row_ is None else row_,
            "col": (z if z_ is None else z_) * 2 + (core if core_ is None else core_),
            "depth": dep if dep_ is None else dep_,
        }

    def along(step):
        return at(z_=lax.rem(z + step + 8, 8))

    def remote(src, dst, send, recv, device):
        return pltpu.make_async_remote_copy(
            src_ref=src, dst_ref=dst, send_sem=send, recv_sem=recv, device_id=device, device_id_type=MESH
        )

    def start(copy):
        copy.start()
        sent.append(copy)

    loads = [
        pltpu.make_async_copy(tok_hbm, tokt, load_sem.at[0]),
        pltpu.make_async_copy(wg_hbm, wg, load_sem.at[1]),
        pltpu.make_async_copy(wu_hbm, wu, load_sem.at[2]),
        pltpu.make_async_copy(gh_hbm.at[0], gh, load_sem.at[3]),
    ]
    for load in loads:
        load.start()

    barrier = pltpu.get_barrier_semaphore()
    peers = [at(row_=lax.rem(row + k, 8)) for k in range(1, 8)]
    beside = row + 1 - 2 * lax.rem(row, 2)
    across = at(row_=beside, dep_=1 - dep)
    peers += [across, at(dep_=1 - dep), along(1), along(-1), at(core_=other)]
    for peer in peers:
        pl.semaphore_signal(barrier, inc=1, device_id=peer, device_id_type=MESH)

    loads[0].wait()
    for m in range(6):
        tok[128 * m : 128 * m + 128, :] = tokt[:, 128 * m : 128 * m + 128].T

    def pack(slot):
        first = pl.multiple_of(lax.rem(z + OFFSETS[slot] + 8, 8) * 96, 32)
        low = tok[pl.ds(first, ROWS), :]
        high = tok[pl.ds(pl.multiple_of(first + ROWS, 16), ROWS), :]
        both = jnp.concatenate([low, high], axis=1)
        pk[slot] = both
        pkr[row, slot] = both

    def tok_copy(m, k, src):
        span = pl.ds(GROUPS[m][0], GROUPS[m][1] - GROUPS[m][0])
        return remote(pk.at[span], pkr.at[src, span], tok_send.at[m, k], tok_recv.at[m, src], at(row_=lax.rem(row + k, 8)))

    def cross_copy():
        return remote(pk, pko.at[row], oth_send.at[0], oth_recv.at[8], across)

    def oth_copy(k, src):
        return remote(pko.at[src], pko.at[src], oth_send.at[k], oth_recv.at[src], at(row_=lax.rem(row + k, 8)))

    def part_copy0(i):
        t0, w = CHUNKS[i]
        return remote(
            part.at[other, 0, :, :, t0 : t0 + w], frm.at[0, :, :, t0 : t0 + w],
            part_send.at[8 + i], part_recv.at[8 + i], at(core_=other),
        )

    def part_copy(slot):
        return remote(part.at[other, slot], frm.at[slot], part_send.at[slot], part_recv.at[slot], at(core_=other))

    def rs_copy(i, way, j):
        d = 0 if way == 1 else 1
        return remote(
            rs_send[i].at[d, j - 1], rs_recv[i].at[d, j - 1], rs_ssem.at[i, d, j - 1], rs_rsem.at[i, d, j - 1], along(way)
        )

    def swap_copy(i):
        return remote(act[i].at[1 - dep], g[i].at[14 + core, 1], swap_send.at[i], swap_recv.at[i], at(dep_=1 - dep))

    def ag_copy(i, way, hop):
        d = 0 if way == 1 else 1
        src = SLOT[-way * (hop - 1)]
        dst = SLOT[-way * hop] if hop < 4 else 0
        return remote(
            g[i].at[2 * src + core], g[i].at[2 * dst + core], ag_send.at[i, d, hop - 1], ag_recv.at[i, d, hop - 1], along(way)
        )

    def fwd_copy(i, slot, whose):
        block = g[i].at[2 * slot + whose]
        return remote(block, block, fwd_send.at[i, slot], fwd_recv.at[i, slot], at(core_=other))

    def unpack(packed, slot, which):
        for m in range(4):
            a = packed[2 * m, slot]
            b = packed[2 * m + 1, slot]
            for c in range(2):
                lanes = slice(64 * c, 64 * c + 64)
                tk[slot, c, which, :, 128 * m : 128 * m + 128] = jnp.concatenate([a[:, lanes], b[:, lanes]], axis=1)

    def project(slots, t0, w):
        lhs = jnp.concatenate([tk[slot, c, 0] for slot in slots for c in range(2)], axis=0)
        for q in range(4):
            first = HALF * (q % 2) + t0
            res = jnp.dot(lhs, (wg, wu)[q // 2][:, first : first + w], preferred_element_type=F32)
            for k, slot in enumerate(slots):
                for c in range(2):
                    rows = ROWS * (2 * k + c)
                    part[c, slot, q, :, t0 : t0 + w] = res[rows : rows + ROWS]

    arrived_parts = set()

    def need_part(slot, i):
        key = slot if slot else 8 + i
        if key not in arrived_parts:
            arrived_parts.add(key)
            (part_copy(slot) if slot else part_copy0(i)).wait_recv()

    def take_tokens(m):
        for k in range(1, 8):
            tok_copy(m, k, lax.rem(row + k, 8)).wait_recv()
        for slot in range(*GROUPS[m]):
            unpack(pkr, slot, 0)

    def step_q(i):
        if i == 0:
            take_tokens(0)
            loads[1].wait()
            loads[2].wait()
        project((0,), *CHUNKS[i])
        start(part_copy0(i))

    def step_p(m):
        take_tokens(m)
        slots = tuple(range(*GROUPS[m]))
        project(slots, 0, HALF)
        for slot in slots:
            start(part_copy(slot))

    def step_x():
        cross_copy().wait_recv()
        for k in range(1, 8):
            start(oth_copy(k, beside))

    unpacked = []

    def step_t(kg):
        if not unpacked:
            for k in range(1, 8):
                oth_copy(k, lax.rem(beside + k, 8)).wait_recv()
        unpacked.append(kg)
        for slot in (2 * kg, 2 * kg + 1):
            unpack(pko, slot, 1)
        rows = tk[2 * kg : 2 * kg + 2].reshape(384, 512)
        for m in range(3):
            tkt[:, 384 * kg + 128 * m : 384 * kg + 128 * m + 128] = rows[128 * m : 128 * m + 128, :].T

    def step_r(i, way, j):
        d = 0 if way == 1 else 1
        slot = SLOT[way * j] if j < 4 else 0
        t0, w = CHUNKS[i]
        arrived = j < HOPS[i][way]
        need_part(slot, i)
        if arrived:
            rs_copy(i, way, j + 1).wait_recv()

        @pl.loop(0, 12)
        def _(it):
            q = it // 3
            rows = pl.ds(pl.multiple_of(it % 3 * 16, 16), 16)
            x = part[core, slot, q, rows, t0 : t0 + w] + frm[slot, q, rows, t0 : t0 + w]
            if arrived:
                x = x + decode(rs_recv[i][d, j, q, rows, :])
            rs_send[i][d, j - 1, q, rows, :] = encode(x)

        start(rs_copy(i, way, j))

    def step_a(i):
        t0, w = CHUNKS[i]
        need_part(7, i)
        rs_copy(i, 1, 1).wait_recv()
        rs_copy(i, -1, 1).wait_recv()
        if loads[3] is not None:
            loads[3].wait()
            loads[3] = None

        def total(q, rows):
            x = part[core, 7, q, rows, t0 : t0 + w] + frm[7, q, rows, t0 : t0 + w]
            return x + decode(rs_recv[i][0, 0, q, rows, :]) + decode(rs_recv[i][1, 0, q, rows, :])

        @pl.loop(0, 3)
        def _(r):
            rows = pl.ds(pl.multiple_of(r * 16, 16), 16)
            for half in range(2):
                cols = slice(HALF * half + t0, HALF * half + t0 + w)
                gate = total(half, rows)
                up = total(2 + half, rows)
                squash = jax.nn.sigmoid(gate)
                hid[0, rows, cols] = (gate * squash * up).astype(BF)
                cot = gh[rows, cols].astype(F32)
                act[i][half, rows, 0:w] = (cot * up * squash * (1.0 + gate * (1.0 - squash))).astype(BF)
                act[i][half, rows, w : 2 * w] = (cot * gate * squash).astype(BF)

        start(swap_copy(i))
        g[i][14 + core, 0] = act[i][dep]

    begun = set()

    def step_n(i, way, hop):
        if hop == 0:
            if i not in begun:
                swap_copy(i).wait_recv()
        else:
            ag_copy(i, way, hop).wait_recv()
        if hop < HOPS[i][way]:
            start(ag_copy(i, way, hop + 1))
        if hop or i not in begun:
            start(fwd_copy(i, SLOT[-way * hop] if hop < 4 else 0, core))
        begun.add(i)

    summed = {}

    def step_w(i, kg):
        t0, w = CHUNKS[i]
        for slot in (2 * kg, 2 * kg + 1):
            fwd_copy(i, slot, other).wait_recv()
        first = i not in summed
        summed[i] = summed.get(i, 0) + 1

        @pl.loop(0, 2)
        def _(half):
            rows = pl.ds(pl.multiple_of(half * 256, 256), 256)
            lhs = tkt[rows, 384 * kg : 384 * kg + 384]
            for tile in range(0, 2 * w // 128, 2):
                rhs = g[i][4 * kg : 4 * kg + 4, :, :, 128 * tile : 128 * tile + 256].reshape(384, 256)
                res = jnp.dot(lhs, rhs, preferred_element_type=F32)
                for k in range(2):
                    out, c = (gg, tile + k) if tile + k < w // 128 else (gu, tile + k - w // 128)
                    cols = slice(t0 + 128 * c, t0 + 128 * c + 128)
                    piece = res[:, 128 * k : 128 * k + 128]
                    out[rows, cols] = piece if first else out[rows, cols] + piece

    for m in range(len(GROUPS)):
        for slot in range(*GROUPS[m]):
            pack(slot)
        if m == 0:
            pl.semaphore_wait(barrier, len(peers))
        for k in range(1, 8):
            start(tok_copy(m, k, row))
    start(cross_copy())
    steps = {"Q": step_q, "P": step_p, "X": step_x, "T": step_t, "R": step_r, "A": step_a, "N": step_n, "W": step_w}
    for name, *args in ORDER:
        steps[name](*args)
    for copy in sent:
        copy.wait_send()


def hand_on(*refs):
    src, dst, sems = refs[:3], refs[3:6], refs[6]
    copies = [pltpu.make_async_copy(src[k], dst[k], sems.at[k]) for k in range(3)]
    for copy in copies:
        copy.start()
    for copy in copies:
        copy.wait()


def local(tokens, gate_weight, up_weight, grad_hidden):
    dma = pltpu.SemaphoreType.DMA
    v = pltpu.VMEM
    any_spec = pl.BlockSpec(memory_space=pl.ANY)
    n = len(CHUNKS)
    widths = [w for _, w in CHUNKS]
    out_shape = (
        jax.ShapeDtypeStruct((1, 48, 1792), BF),
        jax.ShapeDtypeStruct((512, 896), F32),
        jax.ShapeDtypeStruct((512, 896), F32),
    )
    outs = pl.pallas_call(
        kernel,
        out_shape=out_shape,
        in_specs=[pl.BlockSpec(memory_space=pltpu.HBM)] * 4,
        out_specs=(pl.BlockSpec(memory_space=v),) * 3,
        scratch_shapes=[
            v((64, 768), BF), v((768, 64), BF), v((512, 1792), BF), v((512, 1792), BF), v((48, 1792), BF),
            v((8, 48, 128), BF), v((8, 8, 48, 128), BF), v((8, 8, 48, 128), BF),
            v((8, 2, 2, 48, 512), BF), v((512, 1536), BF),
            v((2, 8, 4, 48, 896), F32), v((8, 4, 48, 896), F32),
            *[v((2, 4, 4, 48, w), BF) for w in widths],
            *[v((2, 4, 4, 48, w), BF) for w in widths],
            *[v((2, 48, 2 * w), BF) for w in widths],
            *[v((16, 2, 48, 2 * w), BF) for w in widths],
            dma((4,)), dma((5, 8)), dma((5, 8)), dma((8,)), dma((9,)), dma((8 + n,)), dma((8 + n,)),
            dma((n, 2, 4)), dma((n, 2, 4)), dma((n,)), dma((n,)), dma((n, 2, 4)), dma((n, 2, 4)), dma((n, 8)), dma((n, 8)),
        ],
        compiler_params=pltpu.CompilerParams(collective_id=0, has_side_effects=True, vmem_limit_bytes=46 << 20),
    )(*(pltpu.with_memory_space_constraint(a, pltpu.HBM) for a in (tokens[0].T, gate_weight, up_weight, grad_hidden)))
    return pl.pallas_call(
        hand_on,
        out_shape=out_shape,
        in_specs=[pl.BlockSpec(memory_space=v)] * 3,
        out_specs=(any_spec,) * 3,
        scratch_shapes=[dma((3,))],
        compiler_params=pltpu.CompilerParams(vmem_limit_bytes=8 << 20),
    )(*outs)


def solution(mesh):
    in_specs = (
        P("depth", None, ("col", "row")),
        P("col", "row"),
        P("col", "row"),
        P("depth", "col", "row"),
    )
    out_specs = (P("depth", "col", "row"), P("col", ("row", "depth")), P("col", ("row", "depth")))
    return jax.shard_map(local, mesh=mesh, in_specs=in_specs, out_specs=out_specs, check_vma=False)
```

```python
import jax
import jax.numpy as jnp
from jax import lax
from jax.experimental import pallas as pl
from jax.experimental.pallas import tpu as pltpu
from jax.sharding import PartitionSpec as P

MESH = pl.DeviceIdType.MESH
BF = jnp.bfloat16
F32 = jnp.float32
OFFSETS = (4, 3, -3, 2, -2, 1, -1, 0)
SLOT = {offset: slot for slot, offset in enumerate(OFFSETS)}
GROUPS = ((0, 1), (1, 3), (3, 5), (5, 7), (7, 8))
ROWS = 48
HALF = 896
SCALE = 2.0**18
CHUNKS = ((0, 128), (128, 128), (256, 128), (384, 256), (640, 128), (768, 128))
HOPS = ({1: 4, -1: 3}, {1: 3, -1: 4}, {1: 3, -1: 4}, {1: 3, -1: 4}, {1: 4, -1: 3}, {1: 4, -1: 3})

ORDER = (
    ("Q", 0), ("Q", 1), ("Q", 2), ("Q", 3), ("Q", 4), ("Q", 5), ("R", 0, 1, 4), ("R", 1, -1, 4), ("R", 2, -1, 4),
    ("R", 3, -1, 4), ("R", 4, 1, 4), ("R", 5, 1, 4), ("P", 1), ("P", 2), ("R", 0, 1, 3), ("R", 0, -1, 3),
    ("R", 1, 1, 3), ("R", 1, -1, 3), ("R", 2, 1, 3), ("R", 2, -1, 3), ("R", 3, 1, 3), ("R", 3, -1, 3), ("P", 3),
    ("X",), ("R", 0, 1, 2), ("R", 0, -1, 2), ("R", 1, 1, 2), ("R", 1, -1, 2), ("R", 2, 1, 2), ("R", 2, -1, 2),
    ("R", 3, 1, 2), ("R", 3, -1, 2), ("P", 4), ("R", 0, 1, 1), ("R", 0, -1, 1), ("R", 1, 1, 1), ("R", 1, -1, 1),
    ("R", 2, 1, 1), ("R", 2, -1, 1), ("R", 4, 1, 3), ("R", 4, -1, 3), ("R", 5, 1, 3), ("R", 5, -1, 3),
    ("R", 3, 1, 1), ("R", 3, -1, 1), ("A", 0), ("A", 1), ("A", 2), ("R", 4, 1, 2), ("R", 4, -1, 2), ("R", 5, 1, 2),
    ("R", 5, -1, 2), ("N", 0, 1, 0), ("N", 0, -1, 0), ("N", 1, 1, 0), ("N", 1, -1, 0), ("A", 3), ("N", 2, 1, 0),
    ("N", 2, -1, 0), ("R", 4, 1, 1), ("R", 4, -1, 1), ("R", 5, 1, 1), ("R", 5, -1, 1), ("N", 0, 1, 1),
    ("N", 0, -1, 1), ("N", 1, 1, 1), ("N", 1, -1, 1), ("T", 3), ("N", 2, 1, 1), ("N", 2, -1, 1), ("N", 3, 1, 0),
    ("N", 3, -1, 0), ("T", 2), ("A", 4), ("T", 1), ("A", 5), ("N", 0, 1, 2), ("T", 0), ("N", 0, -1, 2), ("W", 0, 3),
    ("N", 1, 1, 2), ("N", 1, -1, 2), ("W", 0, 2), ("W", 1, 3), ("N", 2, 1, 2), ("W", 2, 3), ("N", 2, -1, 2),
    ("W", 1, 2), ("N", 4, 1, 0), ("N", 4, -1, 0), ("W", 2, 2), ("N", 5, 1, 0), ("N", 5, -1, 0), ("N", 3, 1, 1),
    ("N", 3, -1, 1), ("N", 0, -1, 3), ("W", 3, 3), ("N", 1, 1, 3), ("N", 0, 1, 3), ("N", 1, -1, 3), ("N", 2, 1, 3),
    ("W", 1, 1), ("N", 2, -1, 3), ("W", 0, 1), ("N", 4, 1, 1), ("W", 2, 1), ("N", 4, -1, 1), ("N", 5, 1, 1),
    ("N", 5, -1, 1), ("W", 4, 3), ("W", 5, 3), ("N", 3, 1, 2), ("N", 3, -1, 2), ("N", 0, 1, 4), ("W", 3, 2),
    ("N", 1, -1, 4), ("N", 4, 1, 2), ("W", 0, 0), ("N", 2, -1, 4), ("N", 5, 1, 2), ("W", 1, 0), ("N", 4, -1, 2),
    ("W", 4, 2), ("W", 2, 0), ("N", 5, -1, 2), ("W", 5, 2), ("N", 3, 1, 3), ("N", 4, 1, 3), ("N", 3, -1, 3),
    ("W", 3, 1), ("N", 5, 1, 3), ("W", 4, 1), ("N", 4, -1, 3), ("W", 5, 1), ("N", 5, -1, 3), ("N", 4, 1, 4),
    ("N", 5, 1, 4), ("N", 3, -1, 4), ("W", 4, 0), ("W", 5, 0), ("W", 3, 0),
)


def encode(x):
    t = x * SCALE
    u = t * t
    return (u * t * jnp.abs(t)).astype(BF)


def decode(y):
    y = y.astype(F32)
    r = lax.rsqrt(lax.rsqrt(jnp.abs(y))) * (1.0 / SCALE)
    return jnp.where(y < 0.0, -r, r)


def kernel(tok_hbm, wg_hbm, wu_hbm, gh_hbm, hid, gg, gu, *scratch):
    n = len(CHUNKS)
    (tokt, tok, wg, wu, gh, pk, pkr, pko, tk, tkt, part, frm), scratch = scratch[:12], scratch[12:]
    rs_send, rs_recv, act, g = (scratch[i * n : i * n + n] for i in range(4))
    (
        load_sem, tok_send, tok_recv, oth_send, oth_recv, part_send, part_recv,
        rs_ssem, rs_rsem, swap_send, swap_recv, ag_send, ag_recv, fwd_send, fwd_recv,
    ) = scratch[4 * n :]
    row = lax.axis_index("row")
    col = lax.axis_index("col")
    dep = lax.axis_index("depth")
    z = col // 2
    core = col % 2
    other = 1 - core
    sent = []

    def at(row_=None, z_=None, core_=None, dep_=None):
        return {
            "row": row if row_ is None else row_,
            "col": (z if z_ is None else z_) * 2 + (core if core_ is None else core_),
            "depth": dep if dep_ is None else dep_,
        }

    def along(step):
        return at(z_=lax.rem(z + step + 8, 8))

    def remote(src, dst, send, recv, device):
        return pltpu.make_async_remote_copy(
            src_ref=src, dst_ref=dst, send_sem=send, recv_sem=recv, device_id=device, device_id_type=MESH
        )

    def start(copy):
        copy.start()
        sent.append(copy)

    loads = [
        pltpu.make_async_copy(tok_hbm, tokt, load_sem.at[0]),
        pltpu.make_async_copy(wg_hbm, wg, load_sem.at[1]),
        pltpu.make_async_copy(wu_hbm, wu, load_sem.at[2]),
        pltpu.make_async_copy(gh_hbm.at[0], gh, load_sem.at[3]),
    ]
    for load in loads:
        load.start()

    barrier = pltpu.get_barrier_semaphore()
    peers = [at(row_=lax.rem(row + k, 8)) for k in range(1, 8)]
    beside = row + 1 - 2 * lax.rem(row, 2)
    across = at(row_=beside, dep_=1 - dep)
    peers += [across, at(dep_=1 - dep), along(1), along(-1), at(core_=other)]
    for peer in peers:
        pl.semaphore_signal(barrier, inc=1, device_id=peer, device_id_type=MESH)

    loads[0].wait()
    for m in range(6):
        tok[128 * m : 128 * m + 128, :] = tokt[:, 128 * m : 128 * m + 128].T

    def pack(slot):
        first = pl.multiple_of(lax.rem(z + OFFSETS[slot] + 8, 8) * 96, 32)
        low = tok[pl.ds(first, ROWS), :]
        high = tok[pl.ds(pl.multiple_of(first + ROWS, 16), ROWS), :]
        both = jnp.concatenate([low, high], axis=1)
        pk[slot] = both
        pkr[row, slot] = both

    def tok_copy(m, k, src):
        span = pl.ds(GROUPS[m][0], GROUPS[m][1] - GROUPS[m][0])
        return remote(pk.at[span], pkr.at[src, span], tok_send.at[m, k], tok_recv.at[m, src], at(row_=lax.rem(row + k, 8)))

    def cross_copy():
        return remote(pk, pko.at[row], oth_send.at[0], oth_recv.at[8], across)

    def oth_copy(k, src):
        return remote(pko.at[src], pko.at[src], oth_send.at[k], oth_recv.at[src], at(row_=lax.rem(row + k, 8)))

    def part_copy0(i):
        t0, w = CHUNKS[i]
        return remote(
            part.at[other, 0, :, :, t0 : t0 + w], frm.at[0, :, :, t0 : t0 + w],
            part_send.at[8 + i], part_recv.at[8 + i], at(core_=other),
        )

    def part_copy(slot):
        return remote(part.at[other, slot], frm.at[slot], part_send.at[slot], part_recv.at[slot], at(core_=other))

    def rs_copy(i, way, j):
        d = 0 if way == 1 else 1
        return remote(
            rs_send[i].at[d, j - 1], rs_recv[i].at[d, j - 1], rs_ssem.at[i, d, j - 1], rs_rsem.at[i, d, j - 1], along(way)
        )

    def swap_copy(i):
        return remote(act[i].at[1 - dep], g[i].at[14 + core, 1], swap_send.at[i], swap_recv.at[i], at(dep_=1 - dep))

    def ag_copy(i, way, hop):
        d = 0 if way == 1 else 1
        src = SLOT[-way * (hop - 1)]
        dst = SLOT[-way * hop] if hop < 4 else 0
        return remote(
            g[i].at[2 * src + core], g[i].at[2 * dst + core], ag_send.at[i, d, hop - 1], ag_recv.at[i, d, hop - 1], along(way)
        )

    def fwd_copy(i, slot, whose):
        block = g[i].at[2 * slot + whose]
        return remote(block, block, fwd_send.at[i, slot], fwd_recv.at[i, slot], at(core_=other))

    def unpack(packed, slot, which):
        for m in range(4):
            a = packed[2 * m, slot]
            b = packed[2 * m + 1, slot]
            for c in range(2):
                lanes = slice(64 * c, 64 * c + 64)
                tk[slot, c, which, :, 128 * m : 128 * m + 128] = jnp.concatenate([a[:, lanes], b[:, lanes]], axis=1)

    def project(slots, t0, w):
        lhs = jnp.concatenate([tk[slot, c, 0] for slot in slots for c in range(2)], axis=0)
        for q in range(4):
            first = HALF * (q % 2) + t0
            res = jnp.dot(lhs, (wg, wu)[q // 2][:, first : first + w], preferred_element_type=F32)
            for k, slot in enumerate(slots):
                for c in range(2):
                    rows = ROWS * (2 * k + c)
                    part[c, slot, q, :, t0 : t0 + w] = res[rows : rows + ROWS]

    arrived_parts = set()

    def need_part(slot, i):
        key = slot if slot else 8 + i
        if key not in arrived_parts:
            arrived_parts.add(key)
            (part_copy(slot) if slot else part_copy0(i)).wait_recv()

    def take_tokens(m):
        for k in range(1, 8):
            tok_copy(m, k, lax.rem(row + k, 8)).wait_recv()
        for slot in range(*GROUPS[m]):
            unpack(pkr, slot, 0)

    def step_q(i):
        if i == 0:
            take_tokens(0)
            loads[1].wait()
            loads[2].wait()
        project((0,), *CHUNKS[i])
        start(part_copy0(i))

    def step_p(m):
        take_tokens(m)
        slots = tuple(range(*GROUPS[m]))
        project(slots, 0, HALF)
        for slot in slots:
            start(part_copy(slot))

    def step_x():
        cross_copy().wait_recv()
        for k in range(1, 8):
            start(oth_copy(k, beside))

    unpacked = []

    def step_t(kg):
        if not unpacked:
            for k in range(1, 8):
                oth_copy(k, lax.rem(beside + k, 8)).wait_recv()
        unpacked.append(kg)
        for slot in (2 * kg, 2 * kg + 1):
            unpack(pko, slot, 1)
        rows = tk[2 * kg : 2 * kg + 2].reshape(384, 512)
        for m in range(3):
            tkt[:, 384 * kg + 128 * m : 384 * kg + 128 * m + 128] = rows[128 * m : 128 * m + 128, :].T

    def step_r(i, way, j):
        d = 0 if way == 1 else 1
        slot = SLOT[way * j] if j < 4 else 0
        t0, w = CHUNKS[i]
        arrived = j < HOPS[i][way]
        need_part(slot, i)
        if arrived:
            rs_copy(i, way, j + 1).wait_recv()

        @pl.loop(0, 12)
        def _(it):
            q = it // 3
            rows = pl.ds(pl.multiple_of(it % 3 * 16, 16), 16)
            x = part[core, slot, q, rows, t0 : t0 + w] + frm[slot, q, rows, t0 : t0 + w]
            if arrived:
                x = x + decode(rs_recv[i][d, j, q, rows, :])
            rs_send[i][d, j - 1, q, rows, :] = encode(x)

        start(rs_copy(i, way, j))

    def step_a(i):
        t0, w = CHUNKS[i]
        need_part(7, i)
        rs_copy(i, 1, 1).wait_recv()
        rs_copy(i, -1, 1).wait_recv()
        if loads[3] is not None:
            loads[3].wait()
            loads[3] = None

        def total(q, rows):
            x = part[core, 7, q, rows, t0 : t0 + w] + frm[7, q, rows, t0 : t0 + w]
            return x + decode(rs_recv[i][0, 0, q, rows, :]) + decode(rs_recv[i][1, 0, q, rows, :])

        @pl.loop(0, 3)
        def _(r):
            rows = pl.ds(pl.multiple_of(r * 16, 16), 16)
            for half in range(2):
                cols = slice(HALF * half + t0, HALF * half + t0 + w)
                gate = total(half, rows)
                up = total(2 + half, rows)
                squash = jax.nn.sigmoid(gate)
                hid[0, rows, cols] = (gate * squash * up).astype(BF)
                cot = gh[rows, cols].astype(F32)
                act[i][half, rows, 0:w] = (cot * up * squash * (1.0 + gate * (1.0 - squash))).astype(BF)
                act[i][half, rows, w : 2 * w] = (cot * gate * squash).astype(BF)

        start(swap_copy(i))
        g[i][14 + core, 0] = act[i][dep]

    begun = set()

    def step_n(i, way, hop):
        if hop == 0:
            if i not in begun:
                swap_copy(i).wait_recv()
        else:
            ag_copy(i, way, hop).wait_recv()
        if hop < HOPS[i][way]:
            start(ag_copy(i, way, hop + 1))
        if hop or i not in begun:
            start(fwd_copy(i, SLOT[-way * hop] if hop < 4 else 0, core))
        begun.add(i)

    summed = {}

    def step_w(i, kg):
        t0, w = CHUNKS[i]
        for slot in (2 * kg, 2 * kg + 1):
            fwd_copy(i, slot, other).wait_recv()
        first = i not in summed
        summed[i] = summed.get(i, 0) + 1

        @pl.loop(0, 2)
        def _(half):
            rows = pl.ds(pl.multiple_of(half * 256, 256), 256)
            lhs = tkt[rows, 384 * kg : 384 * kg + 384]
            for tile in range(0, 2 * w // 128, 2):
                rhs = g[i][4 * kg : 4 * kg + 4, :, :, 128 * tile : 128 * tile + 256].reshape(384, 256)
                res = jnp.dot(lhs, rhs, preferred_element_type=F32)
                for k in range(2):
                    out, c = (gg, tile + k) if tile + k < w // 128 else (gu, tile + k - w // 128)
                    cols = slice(t0 + 128 * c, t0 + 128 * c + 128)
                    piece = res[:, 128 * k : 128 * k + 128]
                    out[rows, cols] = piece if first else out[rows, cols] + piece

    for m in range(len(GROUPS)):
        for slot in range(*GROUPS[m]):
            pack(slot)
        if m == 0:
            pl.semaphore_wait(barrier, len(peers))
        for k in range(1, 8):
            start(tok_copy(m, k, row))
    start(cross_copy())
    steps = {"Q": step_q, "P": step_p, "X": step_x, "T": step_t, "R": step_r, "A": step_a, "N": step_n, "W": step_w}
    for name, *args in ORDER:
        steps[name](*args)
    for copy in sent:
        copy.wait_send()


def hand_on(*refs):
    src, dst, sems = refs[:3], refs[3:6], refs[6]
    copies = [pltpu.make_async_copy(src[k], dst[k], sems.at[k]) for k in range(3)]
    for copy in copies:
        copy.start()
    for copy in copies:
        copy.wait()


def local(tokens, gate_weight, up_weight, grad_hidden):
    dma = pltpu.SemaphoreType.DMA
    v = pltpu.VMEM
    any_spec = pl.BlockSpec(memory_space=pl.ANY)
    n = len(CHUNKS)
    widths = [w for _, w in CHUNKS]
    out_shape = (
        jax.ShapeDtypeStruct((1, 48, 1792), BF),
        jax.ShapeDtypeStruct((512, 896), F32),
        jax.ShapeDtypeStruct((512, 896), F32),
    )
    outs = pl.pallas_call(
        kernel,
        out_shape=out_shape,
        in_specs=[pl.BlockSpec(memory_space=pltpu.HBM)] * 4,
        out_specs=(pl.BlockSpec(memory_space=v),) * 3,
        scratch_shapes=[
            v((64, 768), BF), v((768, 64), BF), v((512, 1792), BF), v((512, 1792), BF), v((48, 1792), BF),
            v((8, 48, 128), BF), v((8, 8, 48, 128), BF), v((8, 8, 48, 128), BF),
            v((8, 2, 2, 48, 512), BF), v((512, 1536), BF),
            v((2, 8, 4, 48, 896), F32), v((8, 4, 48, 896), F32),
            *[v((2, 4, 4, 48, w), BF) for w in widths],
            *[v((2, 4, 4, 48, w), BF) for w in widths],
            *[v((2, 48, 2 * w), BF) for w in widths],
            *[v((16, 2, 48, 2 * w), BF) for w in widths],
            dma((4,)), dma((5, 8)), dma((5, 8)), dma((8,)), dma((9,)), dma((8 + n,)), dma((8 + n,)),
            dma((n, 2, 4)), dma((n, 2, 4)), dma((n,)), dma((n,)), dma((n, 2, 4)), dma((n, 2, 4)), dma((n, 8)), dma((n, 8)),
        ],
        compiler_params=pltpu.CompilerParams(collective_id=0, has_side_effects=True, vmem_limit_bytes=46 << 20),
    )(*(pltpu.with_memory_space_constraint(a, pltpu.HBM) for a in (tokens[0].T, gate_weight, up_weight, grad_hidden)))
    return pl.pallas_call(
        hand_on,
        out_shape=out_shape,
        in_specs=[pl.BlockSpec(memory_space=v)] * 3,
        out_specs=(any_spec,) * 3,
        scratch_shapes=[dma((3,))],
        compiler_params=pltpu.CompilerParams(vmem_limit_bytes=8 << 20),
    )(*outs)


def solution(mesh):
    in_specs = (
        P("depth", None, ("col", "row")),
        P("col", "row"),
        P("col", "row"),
        P("depth", "col", "row"),
    )
    out_specs = (P("depth", "col", "row"), P("col", ("row", "depth")), P("col", ("row", "depth")))
    return jax.shard_map(local, mesh=mesh, in_specs=in_specs, out_specs=out_specs, check_vma=False)
```
